256 devices in a mesh: base: 16 (over x, z_hi, core), fine: 16 (over z_lo, y).
Axes of the slice: x: 4, y: 4, z: 8 (z_hi: 2, z_lo: 4; z = z_hi * 4 + z_lo), core: 2. Of those that a mesh axis runs over, the one named last changes fastest.
Arguments:
- coarse_level: float32 [9, 128, 256, 128], P(None, 'base', 'fine'), may hold values from -6 to 6
- fine_level: float32 [16, 16, 9, 16, 8, 128], P('base', 'fine'), may hold values from -6 to 6
- box_list: int32 [16, 16, 2], P('base'), may hold values from 0 to 252, as said below
- patch_owner: int32 [16, 16], P('base'), may hold values from 0 to 15, each once within a row
- reaction_table: int32 [9, 2], replicated, may hold values from 0 to 8
- viscosity: float32 [9], replicated, may hold values from 0.01 to 0.08
- reaction_rates: float32 [9], replicated, may hold values from 0.05 to 0.3
Outputs:
- coarse_out: float32 [9, 128, 256, 128], P(None, 'base', 'fine')
- fine_out: float32 [16, 16, 9, 16, 8, 128], P('base', 'fine')
The draws below stay inside these ranges and needn't reach their ends.
Inputs may be any that keep to these rules, and one draw needn't show every extreme that they name: `box_list`: in each group the boxes are disjoint; the first entry is a multiple of 4 and at most 252, the second is 0 or 64; no block of 16 coarse cells along the second dimension holds more than 2 boxes of a group, and some block holds exactly 2 in every group. `patch_owner`: each group's row is a permutation.
All inputs are finite; a program needn't handle non-finite values.
Results may differ from the reference program's by a relative error of at most 0.0003.
Values sent between devices are 32-bit elements; how exact they have to be, the bound alone decides.
A program may use at most 64 MiB of HBM per device.

```python
import math
import jax
import jax.numpy as jnp
from jax import lax

F = 9
CX = 8
CY = 16
NZ = 128
BY = 4
BZ = 64
FX = 16
FY = 8
NX = 128
NY = 256
N_BASE = 16
N_FINE = 16


def draw_box_list(key, part):

    def one_group(group_key):
        sub_keys = jax.random.split(group_key, 4)
        middle = jax.random.permutation(sub_keys[0], N_FINE - 2) + 1
        blocks = jnp.concatenate([jnp.array([N_FINE - 1, 0], dtype=jnp.int32), middle.astype(jnp.int32)])
        doubled = jax.random.randint(sub_keys[1], (), 1, N_FINE // 2 + 1)
        block_rank = jnp.arange(N_FINE, dtype=jnp.int32)
        counts = jnp.where(block_rank < doubled, 2, jnp.where(block_rank < N_FINE - doubled, 1, 0))
        candidates = jnp.arange(2 * N_FINE, dtype=jnp.int32)
        cand_rank = candidates // 2
        cand_turn = candidates % 2
        is_live = cand_turn < counts[cand_rank]
        scores = jnp.where(is_live, 0, 2 * N_FINE) + candidates
        chosen = jnp.argsort(scores)[:N_FINE]
        slot_count = CY // BY * 2
        raw_perm = jax.vmap(lambda sub_key: jax.random.permutation(sub_key, slot_count))(jax.random.split(sub_keys[2], N_FINE))
        block_ids = jnp.arange(N_FINE, dtype=jnp.int32)
        first_value = jnp.where(block_ids == N_FINE - 1, slot_count - 1, jnp.where(block_ids == 0, 0, raw_perm[:, 0]))
        slot_perm = (raw_perm + (first_value - raw_perm[:, 0])[:, None]) % slot_count
        chosen_block = blocks[cand_rank[chosen]]
        chosen_slot = slot_perm[chosen_block, cand_turn[chosen]]
        y_cell = chosen_block * CY + chosen_slot % (CY // BY) * BY
        z_cell = chosen_slot // (CY // BY) * BZ
        corners = jnp.stack([y_cell, z_cell], axis=1)
        shuffle = jax.random.permutation(sub_keys[3], N_FINE)
        return corners[shuffle].astype(jnp.int32)
    return jax.vmap(one_group)(jax.random.split(key, N_BASE))


def with_ends(drawn, stream_key, smallest, high):
    longest = drawn.shape.index(max(drawn.shape))
    spots = []
    for shift in (0, 1):
        where = [jax.random.randint(jax.random.fold_in(stream_key, axis), (), 0, length) for axis, length in enumerate(drawn.shape)]
        where[longest] = (where[longest] + shift) % drawn.shape[longest]
        spots.append(tuple(where))
    return drawn.at[spots[0]].set(smallest).at[spots[1]].set(high)


def steps_of(own_key, shape, cuts, low, largest):
    level = 1.0
    for axis_at, parts in cuts:
        draws = jax.random.uniform(jax.random.fold_in(jax.random.fold_in(own_key, 6), axis_at), (parts,), jnp.float32, low / len(cuts), largest / len(cuts))
        level = level * jnp.repeat(jnp.exp(draws), shape[axis_at] // parts).reshape((-1,) + (1,) * (len(shape) - 1 - axis_at))
    return level


def centred(own_key, shape, scale, reach, shards=(), kind=jnp.bfloat16):
    gain = steps_of(own_key, shape, shards, -0.22, 0.18) if shards else 1.0
    entries = jax.random.normal(own_key, shape, jnp.float32) * scale * gain
    return jnp.minimum(jnp.maximum(entries, -reach), reach).astype(kind)


def setup_inputs(seed: int = 0) -> dict:
    key_of = jax.random.split(jax.random.key(seed), 8)
    coarse_level = centred(key_of[0], (F, NX, NY, NZ), 1.0, 6.0, ((1, 16), (2, 16)), jnp.float32)
    fine_level = centred(key_of[1], (N_BASE, N_FINE, F, FX, FY, NZ), 1.0, 6.0, ((0, 16), (1, 16)), jnp.float32)
    box_list = draw_box_list(jax.random.fold_in(key_of[7], 71), 0)
    patch_owner = jax.vmap(lambda own: jax.random.permutation(own, N_FINE))(jax.random.split(key_of[3], N_BASE)).reshape((N_BASE, N_FINE)).astype(jnp.int32)
    reaction_table = with_ends(jax.random.randint(key_of[4], (F, 2), 0, F), jax.random.fold_in(key_of[4], 1), 0, F - 1).astype(jnp.int32)
    viscosity = jnp.clip(jnp.exp(jax.random.uniform(key_of[5], (F,), jnp.float32, math.log(0.01), math.log(0.08))), 0.01, 0.08)
    reaction_rates = jnp.clip(jnp.exp(jax.random.uniform(key_of[6], (F,), jnp.float32, math.log(0.05), math.log(0.3))), 0.05, 0.3)
    return dict(coarse_level=coarse_level, fine_level=fine_level, box_list=box_list, patch_owner=patch_owner, reaction_table=reaction_table, viscosity=viscosity, reaction_rates=reaction_rates)


def field_select(reaction_table, fields):
    levels = lax.broadcasted_iota(jnp.int32, (fields, fields), 1)
    pick_left = (reaction_table[:, 0:1] == levels).astype(jnp.float32)
    pick_right = (reaction_table[:, 1:2] == levels).astype(jnp.float32)
    return pick_left, pick_right


def reaction(values, reaction_rates, pick_left, pick_right):
    left_term = jnp.einsum("fg,gxyz->fxyz", pick_left, values, precision=lax.Precision.HIGHEST)
    right_term = jnp.einsum("fg,gxyz->fxyz", pick_right, values, precision=lax.Precision.HIGHEST)
    return reaction_rates[:, None, None, None] * left_term * right_term


def coarse_advance(centre, neighbours, viscosity, reaction_rates, pick_left, pick_right):
    return centre + viscosity[:, None, None, None] * (neighbours - 6.0 * centre) + reaction(centre, reaction_rates, pick_left, pick_right)


def widen_face(face):
    return jnp.repeat(jnp.repeat(face, 2, axis=1), 2, axis=2)


def fine_advance(fine_box, faces, viscosity, reaction_rates, pick_left, pick_right):
    face_xlo, face_xhi, face_ylo, face_yhi, face_zlo, face_zhi = faces
    low_x = widen_face(face_xlo)[:, None]
    high_x = widen_face(face_xhi)[:, None]
    low_y = widen_face(face_ylo)[:, :, None]
    high_y = widen_face(face_yhi)[:, :, None]
    low_z = widen_face(face_zlo)[:, :, :, None]
    high_z = widen_face(face_zhi)[:, :, :, None]
    pair_x = jnp.concatenate([low_x, fine_box[:, :-1]], axis=1) + jnp.concatenate([fine_box[:, 1:], high_x], axis=1)
    pair_y = jnp.concatenate([low_y, fine_box[:, :, :-1]], axis=2) + jnp.concatenate([fine_box[:, :, 1:], high_y], axis=2)
    pair_z = jnp.concatenate([low_z, fine_box[:, :, :, :-1]], axis=3) + jnp.concatenate([fine_box[:, :, :, 1:], high_z], axis=3)
    neighbours = pair_x + pair_y + pair_z
    return fine_box + 2.0 * viscosity[:, None, None, None] * (neighbours - 6.0 * fine_box) + 0.5 * reaction(fine_box, reaction_rates, pick_left, pick_right)


def coarsen(fine_box):
    fields, cells_x, cells_y, cells_z = fine_box.shape
    blocks = fine_box.reshape(fields, cells_x // 2, 2, cells_y // 2, 2, cells_z // 2, 2)
    return 0.125 * jnp.sum(blocks, axis=(2, 4, 6))


def faces_at(coarse_level, group_id, y_cell, z_cell):
    rows_x = (group_id * CX - 1 + jnp.arange(CX + 2, dtype=jnp.int32)) % NX
    rows_y = (y_cell - 1 + jnp.arange(BY + 2, dtype=jnp.int32)) % NY
    rows_z = (z_cell - 1 + jnp.arange(BZ + 2, dtype=jnp.int32)) % NZ
    window = jnp.take(coarse_level, rows_x, axis=1)
    window = jnp.take(window, rows_y, axis=2)
    window = jnp.take(window, rows_z, axis=3)
    return (window[:, 0, 1:-1, 1:-1], window[:, -1, 1:-1, 1:-1], window[:, 1:-1, 0, 1:-1], window[:, 1:-1, -1, 1:-1], window[:, 1:-1, 1:-1, 0], window[:, 1:-1, 1:-1, -1])


def reference(coarse_level, fine_level, box_list, patch_owner, reaction_table, viscosity, reaction_rates):
    pick_left, pick_right = field_select(reaction_table, F)
    neighbours = (jnp.roll(coarse_level, 1, 1) + jnp.roll(coarse_level, -1, 1)) + (jnp.roll(coarse_level, 1, 2) + jnp.roll(coarse_level, -1, 2)) + (jnp.roll(coarse_level, 1, 3) + jnp.roll(coarse_level, -1, 3))
    coarse_next = coarse_advance(coarse_level, neighbours, viscosity, reaction_rates, pick_left, pick_right)

    def one_box(box_index):
        group_id = box_index // N_FINE
        patch_id = box_index % N_FINE
        y_cell = box_list[group_id, patch_id, 0]
        z_cell = box_list[group_id, patch_id, 1]
        fine_box = fine_level[group_id, patch_owner[group_id, patch_id]]
        old_faces = faces_at(coarse_level, group_id, y_cell, z_cell)
        new_faces = faces_at(coarse_next, group_id, y_cell, z_cell)
        mid_faces = tuple(0.5 * (old_face + new_face) for old_face, new_face in zip(old_faces, new_faces))
        fine_box = fine_advance(fine_box, old_faces, viscosity, reaction_rates, pick_left, pick_right)
        fine_box = fine_advance(fine_box, mid_faces, viscosity, reaction_rates, pick_left, pick_right)
        return fine_box, coarsen(fine_box)

    new_boxes, averages = lax.map(one_box, jnp.arange(N_BASE * N_FINE, dtype=jnp.int32))
    groups = jnp.arange(N_BASE, dtype=jnp.int32)[:, None]
    fine_out = jnp.zeros_like(fine_level).at[groups, patch_owner].set(new_boxes.reshape(fine_level.shape))

    def place_mean(box_index, coarse_state):
        box_index = jnp.asarray(box_index).astype(jnp.int32)
        group_id = box_index // N_FINE
        patch_id = box_index % N_FINE
        corner = (jnp.asarray(0).astype(jnp.int32), (group_id * CX).astype(jnp.int32), box_list[group_id, patch_id, 0].astype(jnp.int32), box_list[group_id, patch_id, 1].astype(jnp.int32))
        return lax.dynamic_update_slice(coarse_state, averages[box_index], corner)

    coarse_out = lax.fori_loop(0, N_BASE * N_FINE, place_mean, coarse_next)
    return coarse_out, fine_out
```

```python
import jax
import jax.numpy as jnp
from jax import lax
from jax.sharding import PartitionSpec as P

BY = 4
MOST = 2
BZ = 64


def with_halo(block, sides, width):
    for axis, dim in sides:
        count = lax.axis_size(axis)
        forward = [(i, i + 1) for i in range(count - 1)]
        forward.append((count - 1, 0))
        backward = [(target, source) for source, target in forward]
        low = lax.ppermute(
            lax.slice_in_dim(block, block.shape[dim] - width, None, axis=dim), axis, forward
        )
        high = lax.ppermute(lax.slice_in_dim(block, 0, width, axis=dim), axis, backward)
        block = jnp.concatenate([low, block, high], axis=dim)
    return block


def reaction(values, reaction_rates, left_ids, right_ids):
    fields = values.shape[0]
    left_term = jnp.concatenate(
        [lax.dynamic_slice_in_dim(values, left_ids[f], 1, axis=0) for f in range(fields)]
    )
    right_term = jnp.concatenate(
        [lax.dynamic_slice_in_dim(values, right_ids[f], 1, axis=0) for f in range(fields)]
    )
    return reaction_rates[:, None, None, None] * left_term * right_term


def coarse_advance(centre, neighbours, viscosity, reaction_rates, left_ids, right_ids):
    return (
        centre
        + viscosity[:, None, None, None] * (neighbours - 6.0 * centre)
        + reaction(centre, reaction_rates, left_ids, right_ids)
    )


def widen_face(face):
    return jnp.repeat(jnp.repeat(face, 2, axis=1), 2, axis=2)


def fine_advance(fine_box, faces, viscosity, reaction_rates, left_ids, right_ids):
    face_xlo, face_xhi, face_ylo, face_yhi, face_zlo, face_zhi = faces
    low_x = widen_face(face_xlo)[:, None]
    high_x = widen_face(face_xhi)[:, None]
    low_y = widen_face(face_ylo)[:, :, None]
    high_y = widen_face(face_yhi)[:, :, None]
    low_z = widen_face(face_zlo)[:, :, :, None]
    high_z = widen_face(face_zhi)[:, :, :, None]
    pair_x = jnp.concatenate([low_x, fine_box[:, :-1]], axis=1) + jnp.concatenate(
        [fine_box[:, 1:], high_x], axis=1
    )
    pair_y = jnp.concatenate([low_y, fine_box[:, :, :-1]], axis=2) + jnp.concatenate(
        [fine_box[:, :, 1:], high_y], axis=2
    )
    cells_z = fine_box.shape[3]
    z_pos = lax.broadcasted_iota(jnp.int32, fine_box.shape, 3)
    below = jnp.where(z_pos == 0, low_z, jnp.roll(fine_box, 1, 3))
    above = jnp.where(z_pos == cells_z - 1, high_z, jnp.roll(fine_box, -1, 3))
    pair_z = below + above
    neighbours = pair_x + pair_y + pair_z
    return (
        fine_box
        + 2.0 * viscosity[:, None, None, None] * (neighbours - 6.0 * fine_box)
        + 0.5 * reaction(fine_box, reaction_rates, left_ids, right_ids)
    )


def coarsen(fine_box):
    fields, cells_x, cells_y, cells_z = fine_box.shape
    pairs_x = fine_box.reshape(fields, cells_x // 2, 2, cells_y, cells_z).sum(axis=2)
    pairs_y = pairs_x.reshape(fields, cells_x // 2, cells_y // 2, 2, cells_z).sum(axis=3)
    pair_z = (
        lax.broadcasted_iota(jnp.int32, (cells_z, cells_z // 2), 0) // 2
        == lax.broadcasted_iota(jnp.int32, (cells_z, cells_z // 2), 1)
    ).astype(jnp.float32)
    summed = jnp.einsum("fxyz,zw->fxyw", pairs_y, pair_z, precision=lax.Precision.HIGHEST)
    return 0.125 * summed


def packed_faces(extended, offset, z_start):
    fields, rows_x, _, cells_z = extended.shape
    window = lax.dynamic_slice(extended, (0, 0, offset, 0), (fields, rows_x, BY + 2, cells_z))
    half = lax.dynamic_slice_in_dim(window, z_start, BZ, axis=3)
    low_x = half[:, 0, 1:-1, :]
    high_x = half[:, -1, 1:-1, :]
    low_y = half[:, 1:-1, 0, :]
    high_y = half[:, 1:-1, -1, :]
    inner = window[:, 1:-1, 1:-1, :]
    low_z = lax.dynamic_index_in_dim(inner, (z_start - 1) % cells_z, 3, keepdims=False)
    high_z = lax.dynamic_index_in_dim(inner, (z_start + BZ) % cells_z, 3, keepdims=False)
    return jnp.concatenate(
        [
            face_part.reshape(fields, -1)
            for face_part in (low_x, high_x, low_y, high_y, low_z, high_z)
        ],
        axis=1,
    )


def unpack_faces(packed, cells_x):
    fields = packed.shape[0]
    widths = [BY * BZ, BY * BZ, cells_x * BZ, cells_x * BZ, cells_x * BY, cells_x * BY]
    shapes = [
        (fields, BY, BZ),
        (fields, BY, BZ),
        (fields, cells_x, BZ),
        (fields, cells_x, BZ),
        (fields, cells_x, BY),
        (fields, cells_x, BY),
    ]
    face_list = []
    offset = 0
    for width_now, shape_now in zip(widths, shapes):
        face_list.append(packed[:, offset : offset + width_now].reshape(shape_now))
        offset = offset + width_now
    return tuple(face_list)


def per_device(
    coarse_level, fine_level, box_list, patch_owner, reaction_table, viscosity, reaction_rates
):
    fields, cells_x, height, cells_z = coarse_level.shape
    devices_fine = lax.axis_size("fine")
    my_index = lax.axis_index("fine")
    left_ids = reaction_table[:, 0]
    right_ids = reaction_table[:, 1]

    def extend(coarse_state):
        return with_halo(coarse_state, (("base", 1), ("fine", 2)), 1)

    corners = box_list[0]
    owners = patch_owner[0]
    y_cell = corners[:, 0]
    z_cell = corners[:, 1]
    y_block = y_cell // height
    row_ids = lax.broadcasted_iota(jnp.int32, (devices_fine, devices_fine), 0)
    col_ids = lax.broadcasted_iota(jnp.int32, (devices_fine, devices_fine), 1)
    holder = jnp.sum(jnp.where(owners[None, :] == row_ids, col_ids, 0), axis=1)
    slot_rank = jnp.sum(
        jnp.where((y_block[:, None] == y_block[None, :]) & (col_ids < row_ids), 1, 0), axis=1
    )
    patch_ids = jnp.arange(devices_fine, dtype=jnp.int32)
    slot_patch = []
    slot_filled = []
    for slot_number in range(MOST):
        is_hit = (y_block == my_index) & (slot_rank == slot_number)
        slot_patch.append(jnp.sum(jnp.where(is_hit, patch_ids, 0)))
        slot_filled.append(jnp.any(is_hit))
    box_of_dest = holder
    dest_here = y_block[box_of_dest] == my_index
    dest_slot = slot_rank[box_of_dest]
    source_of_mine = y_block[holder[my_index]]

    def route_faces(extended):
        slots = []
        for slot_number in range(MOST):
            patch_id = slot_patch[slot_number]
            slots.append(
                packed_faces(extended, y_cell[patch_id] - my_index * height, z_cell[patch_id])
            )
        rows = jnp.where(
            (dest_here & (dest_slot == 0))[:, None],
            slots[0].reshape(1, -1),
            jnp.where(dest_here[:, None], slots[1].reshape(1, -1), 0.0),
        )
        arrived = lax.all_to_all(rows, "fine", 0, 0, tiled=True)
        chosen = lax.dynamic_index_in_dim(arrived, source_of_mine, 0, keepdims=False)
        return chosen.reshape(slots[0].shape)

    old_ext = extend(coarse_level)
    old_shell = route_faces(old_ext)
    centre = old_ext[:, 1:-1, 1:-1, :]
    neighbours = (
        old_ext[:, :-2, 1:-1, :]
        + old_ext[:, 2:, 1:-1, :]
        + (old_ext[:, 1:-1, :-2, :] + old_ext[:, 1:-1, 2:, :])
        + (jnp.roll(centre, 1, 3) + jnp.roll(centre, -1, 3))
    )
    coarse_next = coarse_advance(centre, neighbours, viscosity, reaction_rates, left_ids, right_ids)
    new_ext = extend(coarse_next)
    new_shell = route_faces(new_ext)

    fine_box = fine_level[0, 0]
    old_faces = unpack_faces(old_shell, cells_x)
    fine_box = fine_advance(fine_box, old_faces, viscosity, reaction_rates, left_ids, right_ids)
    mid_faces = unpack_faces(0.5 * (old_shell + new_shell), cells_x)
    fine_box = fine_advance(fine_box, mid_faces, viscosity, reaction_rates, left_ids, right_ids)
    averaged = coarsen(fine_box)

    rows_in = lax.all_gather(averaged, "fine", axis=0, tiled=False)
    coarse_out = coarse_next
    for slot_number in range(MOST):
        patch_id = slot_patch[slot_number]
        corner = (0, 0, y_cell[patch_id] - my_index * height, z_cell[patch_id])
        incoming = lax.dynamic_index_in_dim(rows_in, owners[patch_id], 0, keepdims=False)
        present = lax.dynamic_slice(coarse_out, corner, incoming.shape)
        coarse_out = lax.dynamic_update_slice(
            coarse_out, jnp.where(slot_filled[slot_number], incoming, present), corner
        )
    return (coarse_out, fine_box[None, None])


def solution(mesh):
    placed = (
        P(None, "base", "fine", None),
        P("base", "fine", None, None, None, None),
        P("base", None, None),
        P("base", None),
        P(),
        P(),
        P(),
    )
    return jax.shard_map(
        per_device,
        mesh=mesh,
        in_specs=placed,
        out_specs=(P(None, "base", "fine", None), P("base", "fine", None, None, None, None)),
        check_vma=False,
    )
```

```python
import jax
import jax.numpy as jnp
from jax import lax
from jax.sharding import PartitionSpec as P

BY = 4
MOST = 2
BZ = 64


def with_halo(block, sides, width):
    for axis, dim in sides:
        count = lax.axis_size(axis)
        forward = [(i, i + 1) for i in range(count - 1)]
        forward.append((count - 1, 0))
        backward = [(target, source) for source, target in forward]
        low = lax.ppermute(
            lax.slice_in_dim(block, block.shape[dim] - width, None, axis=dim), axis, forward
        )
        high = lax.ppermute(lax.slice_in_dim(block, 0, width, axis=dim), axis, backward)
        block = jnp.concatenate([low, block, high], axis=dim)
    return block


def reaction(values, reaction_rates, left_ids, right_ids):
    fields = values.shape[0]
    levels = lax.broadcasted_iota(jnp.int32, (fields, fields), 1)
    pick_left = (left_ids[:, None] == levels).astype(jnp.float32)
    pick_right = (right_ids[:, None] == levels).astype(jnp.float32)
    left_term = jnp.einsum("fg,gxyz->fxyz", pick_left, values, precision=lax.Precision.HIGHEST)
    right_term = jnp.einsum("fg,gxyz->fxyz", pick_right, values, precision=lax.Precision.HIGHEST)
    return reaction_rates[:, None, None, None] * left_term * right_term


def coarse_advance(centre, neighbours, viscosity, reaction_rates, left_ids, right_ids):
    return (
        centre
        + viscosity[:, None, None, None] * (neighbours - 6.0 * centre)
        + reaction(centre, reaction_rates, left_ids, right_ids)
    )


def widen_face(face):
    return jnp.repeat(jnp.repeat(face, 2, axis=1), 2, axis=2)


def fine_advance(fine_box, faces, viscosity, reaction_rates, left_ids, right_ids):
    face_xlo, face_xhi, face_ylo, face_yhi, face_zlo, face_zhi = faces
    low_x = widen_face(face_xlo)[:, None]
    high_x = widen_face(face_xhi)[:, None]
    low_y = widen_face(face_ylo)[:, :, None]
    high_y = widen_face(face_yhi)[:, :, None]
    low_z = widen_face(face_zlo)[:, :, :, None]
    high_z = widen_face(face_zhi)[:, :, :, None]
    pair_x = jnp.concatenate([low_x, fine_box[:, :-1]], axis=1) + jnp.concatenate(
        [fine_box[:, 1:], high_x], axis=1
    )
    pair_y = jnp.concatenate([low_y, fine_box[:, :, :-1]], axis=2) + jnp.concatenate(
        [fine_box[:, :, 1:], high_y], axis=2
    )
    cells_z = fine_box.shape[3]
    z_pos = lax.broadcasted_iota(jnp.int32, fine_box.shape, 3)
    below = jnp.where(z_pos == 0, low_z, jnp.roll(fine_box, 1, 3))
    above = jnp.where(z_pos == cells_z - 1, high_z, jnp.roll(fine_box, -1, 3))
    pair_z = below + above
    neighbours = pair_x + pair_y + pair_z
    return (
        fine_box
        + 2.0 * viscosity[:, None, None, None] * (neighbours - 6.0 * fine_box)
        + 0.5 * reaction(fine_box, reaction_rates, left_ids, right_ids)
    )


def coarsen(fine_box):
    fields, cells_x, cells_y, cells_z = fine_box.shape
    pairs_x = fine_box.reshape(fields, cells_x // 2, 2, cells_y, cells_z).sum(axis=2)
    pairs_y = pairs_x.reshape(fields, cells_x // 2, cells_y // 2, 2, cells_z).sum(axis=3)
    pair_z = (
        lax.broadcasted_iota(jnp.int32, (cells_z, cells_z // 2), 0) // 2
        == lax.broadcasted_iota(jnp.int32, (cells_z, cells_z // 2), 1)
    ).astype(jnp.float32)
    summed = jnp.einsum("fxyz,zw->fxyw", pairs_y, pair_z, precision=lax.Precision.HIGHEST)
    return 0.125 * summed


def packed_faces(extended, offset, z_start):
    fields, rows_x, _, cells_z = extended.shape
    window = lax.dynamic_slice(extended, (0, 0, offset, 0), (fields, rows_x, BY + 2, cells_z))
    half = lax.dynamic_slice_in_dim(window, z_start, BZ, axis=3)
    low_x = half[:, 0, 1:-1, :]
    high_x = half[:, -1, 1:-1, :]
    low_y = half[:, 1:-1, 0, :]
    high_y = half[:, 1:-1, -1, :]
    inner = window[:, 1:-1, 1:-1, :]
    low_z = lax.dynamic_index_in_dim(inner, (z_start - 1) % cells_z, 3, keepdims=False)
    high_z = lax.dynamic_index_in_dim(inner, (z_start + BZ) % cells_z, 3, keepdims=False)
    return jnp.concatenate(
        [
            face_part.reshape(fields, -1)
            for face_part in (low_x, high_x, low_y, high_y, low_z, high_z)
        ],
        axis=1,
    )


def unpack_faces(packed, cells_x):
    fields = packed.shape[0]
    widths = [BY * BZ, BY * BZ, cells_x * BZ, cells_x * BZ, cells_x * BY, cells_x * BY]
    shapes = [
        (fields, BY, BZ),
        (fields, BY, BZ),
        (fields, cells_x, BZ),
        (fields, cells_x, BZ),
        (fields, cells_x, BY),
        (fields, cells_x, BY),
    ]
    face_list = []
    offset = 0
    for width_now, shape_now in zip(widths, shapes):
        face_list.append(packed[:, offset : offset + width_now].reshape(shape_now))
        offset = offset + width_now
    return tuple(face_list)


def per_device(
    coarse_level, fine_level, box_list, patch_owner, reaction_table, viscosity, reaction_rates
):
    fields, cells_x, height, cells_z = coarse_level.shape
    devices_fine = lax.axis_size("fine")
    my_index = lax.axis_index("fine")
    left_ids = reaction_table[:, 0]
    right_ids = reaction_table[:, 1]

    def extend(coarse_state):
        return with_halo(coarse_state, (("base", 1), ("fine", 2)), 1)

    corners = box_list[0]
    owners = patch_owner[0]
    y_cell = corners[:, 0]
    z_cell = corners[:, 1]
    y_block = y_cell // height
    row_ids = lax.broadcasted_iota(jnp.int32, (devices_fine, devices_fine), 0)
    col_ids = lax.broadcasted_iota(jnp.int32, (devices_fine, devices_fine), 1)
    holder = jnp.sum(jnp.where(owners[None, :] == row_ids, col_ids, 0), axis=1)
    slot_rank = jnp.sum(
        jnp.where((y_block[:, None] == y_block[None, :]) & (col_ids < row_ids), 1, 0), axis=1
    )
    patch_ids = jnp.arange(devices_fine, dtype=jnp.int32)
    slot_patch = []
    slot_filled = []
    for slot_number in range(MOST):
        is_hit = (y_block == my_index) & (slot_rank == slot_number)
        slot_patch.append(jnp.sum(jnp.where(is_hit, patch_ids, 0)))
        slot_filled.append(jnp.any(is_hit))
    box_of_dest = holder
    dest_here = y_block[box_of_dest] == my_index
    dest_slot = slot_rank[box_of_dest]
    source_of_mine = y_block[holder[my_index]]

    def route_faces(extended):
        slots = []
        for slot_number in range(MOST):
            patch_id = slot_patch[slot_number]
            slots.append(
                packed_faces(extended, y_cell[patch_id] - my_index * height, z_cell[patch_id])
            )
        rows = jnp.where(
            (dest_here & (dest_slot == 0))[:, None],
            slots[0].reshape(1, -1),
            jnp.where(dest_here[:, None], slots[1].reshape(1, -1), 0.0),
        )
        arrived = lax.all_to_all(rows, "fine", 0, 0, tiled=True)
        chosen = lax.dynamic_index_in_dim(arrived, source_of_mine, 0, keepdims=False)
        return chosen.reshape(slots[0].shape)

    old_ext = extend(coarse_level)
    old_shell = route_faces(old_ext)
    centre = old_ext[:, 1:-1, 1:-1, :]
    neighbours = (
        old_ext[:, :-2, 1:-1, :]
        + old_ext[:, 2:, 1:-1, :]
        + (old_ext[:, 1:-1, :-2, :] + old_ext[:, 1:-1, 2:, :])
        + (jnp.roll(centre, 1, 3) + jnp.roll(centre, -1, 3))
    )
    coarse_next = coarse_advance(centre, neighbours, viscosity, reaction_rates, left_ids, right_ids)
    new_ext = extend(coarse_next)
    new_shell = route_faces(new_ext)

    fine_box = fine_level[0, 0]
    old_faces = unpack_faces(old_shell, cells_x)
    fine_box = fine_advance(fine_box, old_faces, viscosity, reaction_rates, left_ids, right_ids)
    mid_faces = unpack_faces(0.5 * (old_shell + new_shell), cells_x)
    fine_box = fine_advance(fine_box, mid_faces, viscosity, reaction_rates, left_ids, right_ids)
    averaged = coarsen(fine_box)

    rows_in = lax.all_gather(averaged.reshape(-1, 128), "fine", axis=0, tiled=False)
    coarse_out = coarse_next
    for slot_number in range(MOST):
        patch_id = slot_patch[slot_number]
        corner = (0, 0, y_cell[patch_id] - my_index * height, z_cell[patch_id])
        incoming = lax.dynamic_index_in_dim(rows_in, owners[patch_id], 0, keepdims=False)
        incoming = incoming.reshape(averaged.shape)
        present = lax.dynamic_slice(coarse_out, corner, incoming.shape)
        coarse_out = lax.dynamic_update_slice(
            coarse_out, jnp.where(slot_filled[slot_number], incoming, present), corner
        )
    return (coarse_out, fine_box[None, None])


def solution(mesh):
    placed = (
        P(None, "base", "fine", None),
        P("base", "fine", None, None, None, None),
        P("base", None, None),
        P("base", None),
        P(),
        P(),
        P(),
    )
    return jax.shard_map(
        per_device,
        mesh=mesh,
        in_specs=placed,
        out_specs=(P(None, "base", "fine", None), P("base", "fine", None, None, None, None)),
        check_vma=False,
    )
```

```python
import jax
import jax.numpy as jnp
from jax import lax
from jax.sharding import PartitionSpec as P

BY = 4
MOST = 2
BZ = 64


def with_halo(block, sides, width):
    for axis, dim in sides:
        count = lax.axis_size(axis)
        forward = [(i, i + 1) for i in range(count - 1)]
        forward.append((count - 1, 0))
        backward = [(target, source) for source, target in forward]
        low = lax.ppermute(
            lax.slice_in_dim(block, block.shape[dim] - width, None, axis=dim), axis, forward
        )
        high = lax.ppermute(lax.slice_in_dim(block, 0, width, axis=dim), axis, backward)
        block = jnp.concatenate([low, block, high], axis=dim)
    return block


def reaction(values, reaction_rates, left_ids, right_ids):
    fields = values.shape[0]
    levels = lax.broadcasted_iota(jnp.int32, (fields, fields), 1)
    pick_left = (left_ids[:, None] == levels).astype(jnp.float32)
    pick_right = (right_ids[:, None] == levels).astype(jnp.float32)
    left_term = jnp.einsum("fg,gxyz->fxyz", pick_left, values, precision=lax.Precision.HIGHEST)
    right_term = jnp.einsum("fg,gxyz->fxyz", pick_right, values, precision=lax.Precision.HIGHEST)
    return reaction_rates[:, None, None, None] * left_term * right_term


def coarse_advance(centre, neighbours, viscosity, reaction_rates, left_ids, right_ids):
    return (
        centre
        + viscosity[:, None, None, None] * (neighbours - 6.0 * centre)
        + reaction(centre, reaction_rates, left_ids, right_ids)
    )


def widen_face(face):
    return jnp.repeat(jnp.repeat(face, 2, axis=1), 2, axis=2)


def fine_advance(fine_box, faces, viscosity, reaction_rates, left_ids, right_ids):
    face_xlo, face_xhi, face_ylo, face_yhi, face_zlo, face_zhi = faces
    low_x = widen_face(face_xlo)[:, None]
    high_x = widen_face(face_xhi)[:, None]
    low_y = widen_face(face_ylo)[:, :, None]
    high_y = widen_face(face_yhi)[:, :, None]
    low_z = widen_face(face_zlo)[:, :, :, None]
    high_z = widen_face(face_zhi)[:, :, :, None]
    pair_x = jnp.concatenate([low_x, fine_box[:, :-1]], axis=1) + jnp.concatenate(
        [fine_box[:, 1:], high_x], axis=1
    )
    pair_y = jnp.concatenate([low_y, fine_box[:, :, :-1]], axis=2) + jnp.concatenate(
        [fine_box[:, :, 1:], high_y], axis=2
    )
    cells_z = fine_box.shape[3]
    z_pos = lax.broadcasted_iota(jnp.int32, fine_box.shape, 3)
    below = jnp.where(z_pos == 0, low_z, jnp.roll(fine_box, 1, 3))
    above = jnp.where(z_pos == cells_z - 1, high_z, jnp.roll(fine_box, -1, 3))
    pair_z = below + above
    neighbours = pair_x + pair_y + pair_z
    return (
        fine_box
        + 2.0 * viscosity[:, None, None, None] * (neighbours - 6.0 * fine_box)
        + 0.5 * reaction(fine_box, reaction_rates, left_ids, right_ids)
    )


def coarsen(fine_box):
    fields, cells_x, cells_y, cells_z = fine_box.shape
    pairs_x = fine_box.reshape(fields, cells_x // 2, 2, cells_y, cells_z).sum(axis=2)
    pairs_y = pairs_x.reshape(fields, cells_x // 2, cells_y // 2, 2, cells_z).sum(axis=3)
    pair_z = (
        lax.broadcasted_iota(jnp.int32, (cells_z, cells_z // 2), 0) // 2
        == lax.broadcasted_iota(jnp.int32, (cells_z, cells_z // 2), 1)
    ).astype(jnp.float32)
    summed = jnp.einsum("fxyz,zw->fxyw", pairs_y, pair_z, precision=lax.Precision.HIGHEST)
    return 0.125 * summed


def packed_faces(extended, offset, z_start):
    fields, rows_x, _, cells_z = extended.shape
    window = lax.dynamic_slice(extended, (0, 0, offset, 0), (fields, rows_x, BY + 2, cells_z))
    half = lax.dynamic_slice_in_dim(window, z_start, BZ, axis=3)
    low_x = half[:, 0, 1:-1, :]
    high_x = half[:, -1, 1:-1, :]
    low_y = half[:, 1:-1, 0, :]
    high_y = half[:, 1:-1, -1, :]
    inner = window[:, 1:-1, 1:-1, :]
    low_z = lax.dynamic_index_in_dim(inner, (z_start - 1) % cells_z, 3, keepdims=False)
    high_z = lax.dynamic_index_in_dim(inner, (z_start + BZ) % cells_z, 3, keepdims=False)
    return jnp.concatenate(
        [
            face_part.reshape(fields, -1)
            for face_part in (low_x, high_x, low_y, high_y, low_z, high_z)
        ],
        axis=1,
    )


def unpack_faces(packed, cells_x):
    fields = packed.shape[0]
    widths = [BY * BZ, BY * BZ, cells_x * BZ, cells_x * BZ, cells_x * BY, cells_x * BY]
    shapes = [
        (fields, BY, BZ),
        (fields, BY, BZ),
        (fields, cells_x, BZ),
        (fields, cells_x, BZ),
        (fields, cells_x, BY),
        (fields, cells_x, BY),
    ]
    face_list = []
    offset = 0
    for width_now, shape_now in zip(widths, shapes):
        face_list.append(packed[:, offset : offset + width_now].reshape(shape_now))
        offset = offset + width_now
    return tuple(face_list)


def per_device(
    coarse_level, fine_level, box_list, patch_owner, reaction_table, viscosity, reaction_rates
):
    fields, cells_x, height, cells_z = coarse_level.shape
    devices_fine = lax.axis_size("fine")
    my_index = lax.axis_index("fine")
    left_ids = reaction_table[:, 0]
    right_ids = reaction_table[:, 1]

    def extend(coarse_state):
        return with_halo(coarse_state, (("base", 1), ("fine", 2)), 1)

    corners = box_list[0]
    owners = patch_owner[0]
    y_cell = corners[:, 0]
    z_cell = corners[:, 1]
    y_block = y_cell // height
    row_ids = lax.broadcasted_iota(jnp.int32, (devices_fine, devices_fine), 0)
    col_ids = lax.broadcasted_iota(jnp.int32, (devices_fine, devices_fine), 1)
    holder = jnp.sum(jnp.where(owners[None, :] == row_ids, col_ids, 0), axis=1)
    slot_rank = jnp.sum(
        jnp.where((y_block[:, None] == y_block[None, :]) & (col_ids < row_ids), 1, 0), axis=1
    )
    patch_ids = jnp.arange(devices_fine, dtype=jnp.int32)
    slot_patch = []
    slot_filled = []
    for slot_number in range(MOST):
        is_hit = (y_block == my_index) & (slot_rank == slot_number)
        slot_patch.append(jnp.sum(jnp.where(is_hit, patch_ids, 0)))
        slot_filled.append(jnp.any(is_hit))
    box_of_dest = holder
    dest_here = y_block[box_of_dest] == my_index
    dest_slot = slot_rank[box_of_dest]
    source_of_mine = y_block[holder[my_index]]

    def route_faces(extended):
        slots = []
        for slot_number in range(MOST):
            patch_id = slot_patch[slot_number]
            slots.append(
                packed_faces(extended, y_cell[patch_id] - my_index * height, z_cell[patch_id])
            )
        rows = jnp.where(
            (dest_here & (dest_slot == 0))[:, None],
            slots[0].reshape(1, -1),
            jnp.where(dest_here[:, None], slots[1].reshape(1, -1), 0.0),
        )
        arrived = lax.all_to_all(rows, "fine", 0, 0, tiled=True)
        chosen = lax.dynamic_index_in_dim(arrived, source_of_mine, 0, keepdims=False)
        return chosen.reshape(slots[0].shape)

    old_ext = extend(coarse_level)
    old_shell = route_faces(old_ext)
    centre = old_ext[:, 1:-1, 1:-1, :]
    neighbours = (
        old_ext[:, :-2, 1:-1, :]
        + old_ext[:, 2:, 1:-1, :]
        + (old_ext[:, 1:-1, :-2, :] + old_ext[:, 1:-1, 2:, :])
        + (jnp.roll(centre, 1, 3) + jnp.roll(centre, -1, 3))
    )
    coarse_next = coarse_advance(centre, neighbours, viscosity, reaction_rates, left_ids, right_ids)
    new_ext = extend(coarse_next)
    new_shell = route_faces(new_ext)

    fine_box = fine_level[0, 0]
    old_faces = unpack_faces(old_shell, cells_x)
    fine_box = fine_advance(fine_box, old_faces, viscosity, reaction_rates, left_ids, right_ids)
    mid_faces = unpack_faces(0.5 * (old_shell + new_shell), cells_x)
    fine_box = fine_advance(fine_box, mid_faces, viscosity, reaction_rates, left_ids, right_ids)
    averaged = coarsen(fine_box)

    dest_ids = lax.broadcasted_iota(jnp.int32, (devices_fine, 1), 0)
    sent = jnp.where(dest_ids == source_of_mine, averaged.reshape(1, -1), 0.0)
    rows_in = lax.all_to_all(sent, "fine", 0, 0, tiled=True)
    coarse_out = coarse_next
    for slot_number in range(MOST):
        patch_id = slot_patch[slot_number]
        corner = (0, 0, y_cell[patch_id] - my_index * height, z_cell[patch_id])
        incoming = lax.dynamic_index_in_dim(rows_in, owners[patch_id], 0, keepdims=False)
        incoming = incoming.reshape(averaged.shape)
        present = lax.dynamic_slice(coarse_out, corner, incoming.shape)
        coarse_out = lax.dynamic_update_slice(
            coarse_out, jnp.where(slot_filled[slot_number], incoming, present), corner
        )
    return (coarse_out, fine_box[None, None])


def solution(mesh):
    placed = (
        P(None, "base", "fine", None),
        P("base", "fine", None, None, None, None),
        P("base", None, None),
        P("base", None),
        P(),
        P(),
        P(),
    )
    return jax.shard_map(
        per_device,
        mesh=mesh,
        in_specs=placed,
        out_specs=(P(None, "base", "fine", None), P("base", "fine", None, None, None, None)),
        check_vma=False,
    )
```

```python
import jax
import jax.numpy as jnp
from jax import lax
from jax.sharding import PartitionSpec as P

BY = 4
MOST = 2
BZ = 64


def ring_pairs(axis):
    count = lax.axis_size(axis)
    forward = [(i, (i + 1) % count) for i in range(count)]
    backward = [(target, source) for source, target in forward]
    return forward, backward


def with_halo(block):
    x_forward, x_backward = ring_pairs("base")
    y_forward, y_backward = ring_pairs("fine")
    low_x = lax.ppermute(block[:, -1:], "base", x_forward)
    high_x = lax.ppermute(block[:, :1], "base", x_backward)
    low_y = lax.ppermute(block[:, :, -1:], "fine", y_forward)
    high_y = lax.ppermute(block[:, :, :1], "fine", y_backward)
    corner = jnp.zeros_like(block[:, :1, :1])
    low_y = jnp.concatenate([corner, low_y, corner], axis=1)
    high_y = jnp.concatenate([corner, high_y, corner], axis=1)
    block = jnp.concatenate([low_x, block, high_x], axis=1)
    return jnp.concatenate([low_y, block, high_y], axis=2)


def reaction(values, reaction_rates, left_ids, right_ids):
    fields = values.shape[0]
    levels = lax.broadcasted_iota(jnp.int32, (fields, fields), 1)
    pick_left = (left_ids[:, None] == levels).astype(jnp.float32)
    pick_right = (right_ids[:, None] == levels).astype(jnp.float32)
    left_term = jnp.einsum("fg,gxyz->fxyz", pick_left, values, precision=lax.Precision.HIGHEST)
    right_term = jnp.einsum("fg,gxyz->fxyz", pick_right, values, precision=lax.Precision.HIGHEST)
    return reaction_rates[:, None, None, None] * left_term * right_term


def coarse_advance(centre, neighbours, viscosity, reaction_rates, left_ids, right_ids):
    return (
        centre
        + viscosity[:, None, None, None] * (neighbours - 6.0 * centre)
        + reaction(centre, reaction_rates, left_ids, right_ids)
    )


def widen_face(face):
    return jnp.repeat(jnp.repeat(face, 2, axis=1), 2, axis=2)


def fine_advance(fine_box, faces, viscosity, reaction_rates, left_ids, right_ids):
    face_xlo, face_xhi, face_ylo, face_yhi, face_zlo, face_zhi = faces
    low_x = widen_face(face_xlo)[:, None]
    high_x = widen_face(face_xhi)[:, None]
    low_y = widen_face(face_ylo)[:, :, None]
    high_y = widen_face(face_yhi)[:, :, None]
    low_z = widen_face(face_zlo)[:, :, :, None]
    high_z = widen_face(face_zhi)[:, :, :, None]
    pair_x = jnp.concatenate([low_x, fine_box[:, :-1]], axis=1) + jnp.concatenate(
        [fine_box[:, 1:], high_x], axis=1
    )
    pair_y = jnp.concatenate([low_y, fine_box[:, :, :-1]], axis=2) + jnp.concatenate(
        [fine_box[:, :, 1:], high_y], axis=2
    )
    cells_z = fine_box.shape[3]
    z_pos = lax.broadcasted_iota(jnp.int32, fine_box.shape, 3)
    below = jnp.where(z_pos == 0, low_z, jnp.roll(fine_box, 1, 3))
    above = jnp.where(z_pos == cells_z - 1, high_z, jnp.roll(fine_box, -1, 3))
    pair_z = below + above
    neighbours = pair_x + pair_y + pair_z
    return (
        fine_box
        + 2.0 * viscosity[:, None, None, None] * (neighbours - 6.0 * fine_box)
        + 0.5 * reaction(fine_box, reaction_rates, left_ids, right_ids)
    )


def coarsen(fine_box):
    fields, cells_x, cells_y, cells_z = fine_box.shape
    pairs_x = fine_box.reshape(fields, cells_x // 2, 2, cells_y, cells_z).sum(axis=2)
    pairs_y = pairs_x.reshape(fields, cells_x // 2, cells_y // 2, 2, cells_z).sum(axis=3)
    pair_z = (
        lax.broadcasted_iota(jnp.int32, (cells_z, cells_z // 2), 0) // 2
        == lax.broadcasted_iota(jnp.int32, (cells_z, cells_z // 2), 1)
    ).astype(jnp.float32)
    summed = jnp.einsum("fxyz,zw->fxyw", pairs_y, pair_z, precision=lax.Precision.HIGHEST)
    return 0.125 * summed


def packed_faces(extended, offset, z_start):
    fields, rows_x, _, cells_z = extended.shape
    window = lax.dynamic_slice(extended, (0, 0, offset, 0), (fields, rows_x, BY + 2, cells_z))
    half = lax.dynamic_slice_in_dim(window, z_start, BZ, axis=3)
    low_x = half[:, 0, 1:-1, :]
    high_x = half[:, -1, 1:-1, :]
    low_y = half[:, 1:-1, 0, :]
    high_y = half[:, 1:-1, -1, :]
    inner = window[:, 1:-1, 1:-1, :]
    low_z = lax.dynamic_index_in_dim(inner, (z_start - 1) % cells_z, 3, keepdims=False)
    high_z = lax.dynamic_index_in_dim(inner, (z_start + BZ) % cells_z, 3, keepdims=False)
    return jnp.concatenate(
        [
            face_part.reshape(fields, -1)
            for face_part in (low_x, high_x, low_y, high_y, low_z, high_z)
        ],
        axis=1,
    )


def unpack_faces(packed, cells_x):
    fields = packed.shape[0]
    widths = [BY * BZ, BY * BZ, cells_x * BZ, cells_x * BZ, cells_x * BY, cells_x * BY]
    shapes = [
        (fields, BY, BZ),
        (fields, BY, BZ),
        (fields, cells_x, BZ),
        (fields, cells_x, BZ),
        (fields, cells_x, BY),
        (fields, cells_x, BY),
    ]
    face_list = []
    offset = 0
    for width_now, shape_now in zip(widths, shapes):
        face_list.append(packed[:, offset : offset + width_now].reshape(shape_now))
        offset = offset + width_now
    return tuple(face_list)


def per_device(
    coarse_level, fine_level, box_list, patch_owner, reaction_table, viscosity, reaction_rates
):
    fields, cells_x, height, cells_z = coarse_level.shape
    devices_fine = lax.axis_size("fine")
    my_index = lax.axis_index("fine")
    left_ids = reaction_table[:, 0]
    right_ids = reaction_table[:, 1]

    corners = box_list[0]
    owners = patch_owner[0]
    y_cell = corners[:, 0]
    z_cell = corners[:, 1]
    y_block = y_cell // height
    row_ids = lax.broadcasted_iota(jnp.int32, (devices_fine, devices_fine), 0)
    col_ids = lax.broadcasted_iota(jnp.int32, (devices_fine, devices_fine), 1)
    holder = jnp.sum(jnp.where(owners[None, :] == row_ids, col_ids, 0), axis=1)
    slot_rank = jnp.sum(
        jnp.where((y_block[:, None] == y_block[None, :]) & (col_ids < row_ids), 1, 0), axis=1
    )
    patch_ids = jnp.arange(devices_fine, dtype=jnp.int32)
    slot_patch = []
    slot_filled = []
    for slot_number in range(MOST):
        is_hit = (y_block == my_index) & (slot_rank == slot_number)
        slot_patch.append(jnp.sum(jnp.where(is_hit, patch_ids, 0)))
        slot_filled.append(jnp.any(is_hit))
    box_of_dest = holder
    dest_here = y_block[box_of_dest] == my_index
    dest_slot = slot_rank[box_of_dest]
    source_of_mine = y_block[holder[my_index]]

    def slot_faces(extended, slot_number):
        patch_id = slot_patch[slot_number]
        return packed_faces(extended, y_cell[patch_id] - my_index * height, z_cell[patch_id])

    old_ext = with_halo(coarse_level)
    centre = old_ext[:, 1:-1, 1:-1, :]
    neighbours = (
        old_ext[:, :-2, 1:-1, :]
        + old_ext[:, 2:, 1:-1, :]
        + (old_ext[:, 1:-1, :-2, :] + old_ext[:, 1:-1, 2:, :])
        + (jnp.roll(centre, 1, 3) + jnp.roll(centre, -1, 3))
    )
    coarse_next = coarse_advance(centre, neighbours, viscosity, reaction_rates, left_ids, right_ids)
    new_ext = with_halo(coarse_next)
    slots = [
        jnp.stack([slot_faces(old_ext, slot_number), slot_faces(new_ext, slot_number)])
        for slot_number in range(MOST)
    ]
    rows = jnp.where(
        (dest_here & (dest_slot == 0))[:, None],
        slots[0].reshape(1, -1),
        jnp.where(dest_here[:, None], slots[1].reshape(1, -1), 0.0),
    )
    arrived = lax.all_to_all(rows, "fine", 0, 0, tiled=True)
    shell_pair = lax.dynamic_index_in_dim(arrived, source_of_mine, 0, keepdims=False)
    shell_pair = shell_pair.reshape(slots[0].shape)
    old_shell = shell_pair[0]
    new_shell = shell_pair[1]

    fine_box = fine_level[0, 0]
    old_faces = unpack_faces(old_shell, cells_x)
    fine_box = fine_advance(fine_box, old_faces, viscosity, reaction_rates, left_ids, right_ids)
    mid_faces = unpack_faces(0.5 * (old_shell + new_shell), cells_x)
    fine_box = fine_advance(fine_box, mid_faces, viscosity, reaction_rates, left_ids, right_ids)
    averaged = coarsen(fine_box)

    dest_ids = lax.broadcasted_iota(jnp.int32, (devices_fine, 1), 0)
    sent = jnp.where(dest_ids == source_of_mine, averaged.reshape(1, -1), 0.0)
    rows_in = lax.all_to_all(sent, "fine", 0, 0, tiled=True)
    coarse_out = coarse_next
    for slot_number in range(MOST):
        patch_id = slot_patch[slot_number]
        corner = (0, 0, y_cell[patch_id] - my_index * height, z_cell[patch_id])
        incoming = lax.dynamic_index_in_dim(rows_in, owners[patch_id], 0, keepdims=False)
        incoming = incoming.reshape(averaged.shape)
        present = lax.dynamic_slice(coarse_out, corner, incoming.shape)
        coarse_out = lax.dynamic_update_slice(
            coarse_out, jnp.where(slot_filled[slot_number], incoming, present), corner
        )
    return (coarse_out, fine_box[None, None])


def solution(mesh):
    placed = (
        P(None, "base", "fine", None),
        P("base", "fine", None, None, None, None),
        P("base", None, None),
        P("base", None),
        P(),
        P(),
        P(),
    )
    return jax.shard_map(
        per_device,
        mesh=mesh,
        in_specs=placed,
        out_specs=(P(None, "base", "fine", None), P("base", "fine", None, None, None, None)),
        check_vma=False,
    )
```

```python
import jax
import jax.numpy as jnp
from jax import lax
from jax.sharding import PartitionSpec as P

BY = 4
MOST = 2
BZ = 64


def ring_pairs(axis):
    count = lax.axis_size(axis)
    forward = [(i, (i + 1) % count) for i in range(count)]
    backward = [(target, source) for source, target in forward]
    return forward, backward


def diagonal_pairs(step_x, step_y):
    count_x = lax.axis_size("base")
    count_y = lax.axis_size("fine")
    return [
        (
            x * count_y + y,
            ((x + step_x) % count_x) * count_y + (y + step_y) % count_y,
        )
        for x in range(count_x)
        for y in range(count_y)
    ]


def with_deep_halo(block):
    x_forward, x_backward = ring_pairs("base")
    y_forward, y_backward = ring_pairs("fine")
    both = ("base", "fine")
    low_x = lax.ppermute(block[:, -2:], "base", x_forward)
    high_x = lax.ppermute(block[:, :2], "base", x_backward)
    low_y = lax.ppermute(block[:, :, -2:], "fine", y_forward)
    high_y = lax.ppermute(block[:, :, :2], "fine", y_backward)
    low_low = lax.ppermute(block[:, -1:, -1:], both, diagonal_pairs(1, 1))
    low_high = lax.ppermute(block[:, -1:, :1], both, diagonal_pairs(1, -1))
    high_low = lax.ppermute(block[:, :1, -1:], both, diagonal_pairs(-1, 1))
    high_high = lax.ppermute(block[:, :1, :1], both, diagonal_pairs(-1, -1))
    blank = jnp.zeros_like(block[:, :1, :1])
    blank_pair = jnp.zeros_like(block[:, :1, :2])
    middle = jnp.concatenate([low_y, block, high_y], axis=2)
    row_m2 = jnp.concatenate([blank_pair, low_x[:, 0:1], blank_pair], axis=2)
    row_m1 = jnp.concatenate([blank, low_low, low_x[:, 1:2], low_high, blank], axis=2)
    row_p0 = jnp.concatenate([blank, high_low, high_x[:, 0:1], high_high, blank], axis=2)
    row_p1 = jnp.concatenate([blank_pair, high_x[:, 1:2], blank_pair], axis=2)
    return jnp.concatenate([row_m2, row_m1, middle, row_p0, row_p1], axis=1)


def reaction(values, reaction_rates, left_ids, right_ids):
    fields = values.shape[0]
    levels = lax.broadcasted_iota(jnp.int32, (fields, fields), 1)
    pick_left = (left_ids[:, None] == levels).astype(jnp.float32)
    pick_right = (right_ids[:, None] == levels).astype(jnp.float32)
    left_term = jnp.einsum("fg,gxyz->fxyz", pick_left, values, precision=lax.Precision.HIGHEST)
    right_term = jnp.einsum("fg,gxyz->fxyz", pick_right, values, precision=lax.Precision.HIGHEST)
    return reaction_rates[:, None, None, None] * left_term * right_term


def coarse_advance(centre, neighbours, viscosity, reaction_rates, left_ids, right_ids):
    return (
        centre
        + viscosity[:, None, None, None] * (neighbours - 6.0 * centre)
        + reaction(centre, reaction_rates, left_ids, right_ids)
    )


def widen_face(face):
    return jnp.repeat(jnp.repeat(face, 2, axis=1), 2, axis=2)


def fine_advance(fine_box, faces, viscosity, reaction_rates, left_ids, right_ids):
    face_xlo, face_xhi, face_ylo, face_yhi, face_zlo, face_zhi = faces
    low_x = widen_face(face_xlo)[:, None]
    high_x = widen_face(face_xhi)[:, None]
    low_y = widen_face(face_ylo)[:, :, None]
    high_y = widen_face(face_yhi)[:, :, None]
    low_z = widen_face(face_zlo)[:, :, :, None]
    high_z = widen_face(face_zhi)[:, :, :, None]
    pair_x = jnp.concatenate([low_x, fine_box[:, :-1]], axis=1) + jnp.concatenate(
        [fine_box[:, 1:], high_x], axis=1
    )
    pair_y = jnp.concatenate([low_y, fine_box[:, :, :-1]], axis=2) + jnp.concatenate(
        [fine_box[:, :, 1:], high_y], axis=2
    )
    cells_z = fine_box.shape[3]
    z_pos = lax.broadcasted_iota(jnp.int32, fine_box.shape, 3)
    below = jnp.where(z_pos == 0, low_z, jnp.roll(fine_box, 1, 3))
    above = jnp.where(z_pos == cells_z - 1, high_z, jnp.roll(fine_box, -1, 3))
    pair_z = below + above
    neighbours = pair_x + pair_y + pair_z
    return (
        fine_box
        + 2.0 * viscosity[:, None, None, None] * (neighbours - 6.0 * fine_box)
        + 0.5 * reaction(fine_box, reaction_rates, left_ids, right_ids)
    )


def coarsen(fine_box):
    fields, cells_x, cells_y, cells_z = fine_box.shape
    pairs_x = fine_box.reshape(fields, cells_x // 2, 2, cells_y, cells_z).sum(axis=2)
    pairs_y = pairs_x.reshape(fields, cells_x // 2, cells_y // 2, 2, cells_z).sum(axis=3)
    pair_z = (
        lax.broadcasted_iota(jnp.int32, (cells_z, cells_z // 2), 0) // 2
        == lax.broadcasted_iota(jnp.int32, (cells_z, cells_z // 2), 1)
    ).astype(jnp.float32)
    summed = jnp.einsum("fxyz,zw->fxyw", pairs_y, pair_z, precision=lax.Precision.HIGHEST)
    return 0.125 * summed


def packed_faces(extended, offset, z_start):
    fields, rows_x, _, cells_z = extended.shape
    window = lax.dynamic_slice(extended, (0, 0, offset, 0), (fields, rows_x, BY + 2, cells_z))
    half = lax.dynamic_slice_in_dim(window, z_start, BZ, axis=3)
    low_x = half[:, 0, 1:-1, :]
    high_x = half[:, -1, 1:-1, :]
    low_y = half[:, 1:-1, 0, :]
    high_y = half[:, 1:-1, -1, :]
    inner = window[:, 1:-1, 1:-1, :]
    low_z = lax.dynamic_index_in_dim(inner, (z_start - 1) % cells_z, 3, keepdims=False)
    high_z = lax.dynamic_index_in_dim(inner, (z_start + BZ) % cells_z, 3, keepdims=False)
    return jnp.concatenate(
        [
            face_part.reshape(fields, -1)
            for face_part in (low_x, high_x, low_y, high_y, low_z, high_z)
        ],
        axis=1,
    )


def unpack_faces(packed, cells_x):
    fields = packed.shape[0]
    widths = [BY * BZ, BY * BZ, cells_x * BZ, cells_x * BZ, cells_x * BY, cells_x * BY]
    shapes = [
        (fields, BY, BZ),
        (fields, BY, BZ),
        (fields, cells_x, BZ),
        (fields, cells_x, BZ),
        (fields, cells_x, BY),
        (fields, cells_x, BY),
    ]
    face_list = []
    offset = 0
    for width_now, shape_now in zip(widths, shapes):
        face_list.append(packed[:, offset : offset + width_now].reshape(shape_now))
        offset = offset + width_now
    return tuple(face_list)


def per_device(
    coarse_level, fine_level, box_list, patch_owner, reaction_table, viscosity, reaction_rates
):
    fields, cells_x, height, cells_z = coarse_level.shape
    devices_fine = lax.axis_size("fine")
    my_index = lax.axis_index("fine")
    left_ids = reaction_table[:, 0]
    right_ids = reaction_table[:, 1]

    corners = box_list[0]
    owners = patch_owner[0]
    y_cell = corners[:, 0]
    z_cell = corners[:, 1]
    y_block = y_cell // height
    row_ids = lax.broadcasted_iota(jnp.int32, (devices_fine, devices_fine), 0)
    col_ids = lax.broadcasted_iota(jnp.int32, (devices_fine, devices_fine), 1)
    holder = jnp.sum(jnp.where(owners[None, :] == row_ids, col_ids, 0), axis=1)
    slot_rank = jnp.sum(
        jnp.where((y_block[:, None] == y_block[None, :]) & (col_ids < row_ids), 1, 0), axis=1
    )
    patch_ids = jnp.arange(devices_fine, dtype=jnp.int32)
    slot_patch = []
    slot_filled = []
    for slot_number in range(MOST):
        is_hit = (y_block == my_index) & (slot_rank == slot_number)
        slot_patch.append(jnp.sum(jnp.where(is_hit, patch_ids, 0)))
        slot_filled.append(jnp.any(is_hit))
    box_of_dest = holder
    dest_here = y_block[box_of_dest] == my_index
    dest_slot = slot_rank[box_of_dest]
    source_of_mine = y_block[holder[my_index]]

    def slot_faces(extended, slot_number):
        patch_id = slot_patch[slot_number]
        return packed_faces(extended, y_cell[patch_id] - my_index * height, z_cell[patch_id])

    deep = with_deep_halo(coarse_level)
    old_ext = deep[:, 1:-1, 1:-1, :]
    neighbours = (
        deep[:, :-2, 1:-1, :]
        + deep[:, 2:, 1:-1, :]
        + (deep[:, 1:-1, :-2, :] + deep[:, 1:-1, 2:, :])
        + (jnp.roll(old_ext, 1, 3) + jnp.roll(old_ext, -1, 3))
    )
    new_ext = coarse_advance(old_ext, neighbours, viscosity, reaction_rates, left_ids, right_ids)
    coarse_next = new_ext[:, 1:-1, 1:-1, :]
    slots = [
        jnp.stack([slot_faces(old_ext, slot_number), slot_faces(new_ext, slot_number)])
        for slot_number in range(MOST)
    ]
    rows = jnp.where(
        (dest_here & (dest_slot == 0))[:, None],
        slots[0].reshape(1, -1),
        jnp.where(dest_here[:, None], slots[1].reshape(1, -1), 0.0),
    )
    arrived = lax.all_to_all(rows, "fine", 0, 0, tiled=True)
    shell_pair = lax.dynamic_index_in_dim(arrived, source_of_mine, 0, keepdims=False)
    shell_pair = shell_pair.reshape(slots[0].shape)
    old_shell = shell_pair[0]
    new_shell = shell_pair[1]

    fine_box = fine_level[0, 0]
    old_faces = unpack_faces(old_shell, cells_x)
    fine_box = fine_advance(fine_box, old_faces, viscosity, reaction_rates, left_ids, right_ids)
    mid_faces = unpack_faces(0.5 * (old_shell + new_shell), cells_x)
    fine_box = fine_advance(fine_box, mid_faces, viscosity, reaction_rates, left_ids, right_ids)
    averaged = coarsen(fine_box)

    dest_ids = lax.broadcasted_iota(jnp.int32, (devices_fine, 1), 0)
    sent = jnp.where(dest_ids == source_of_mine, averaged.reshape(1, -1), 0.0)
    rows_in = lax.all_to_all(sent, "fine", 0, 0, tiled=True)
    coarse_out = coarse_next
    for slot_number in range(MOST):
        patch_id = slot_patch[slot_number]
        corner = (0, 0, y_cell[patch_id] - my_index * height, z_cell[patch_id])
        incoming = lax.dynamic_index_in_dim(rows_in, owners[patch_id], 0, keepdims=False)
        incoming = incoming.reshape(averaged.shape)
        present = lax.dynamic_slice(coarse_out, corner, incoming.shape)
        coarse_out = lax.dynamic_update_slice(
            coarse_out, jnp.where(slot_filled[slot_number], incoming, present), corner
        )
    return (coarse_out, fine_box[None, None])


def solution(mesh):
    placed = (
        P(None, "base", "fine", None),
        P("base", "fine", None, None, None, None),
        P("base", None, None),
        P("base", None),
        P(),
        P(),
        P(),
    )
    return jax.shard_map(
        per_device,
        mesh=mesh,
        in_specs=placed,
        out_specs=(P(None, "base", "fine", None), P("base", "fine", None, None, None, None)),
        check_vma=False,
    )
```

```python
import jax
import jax.numpy as jnp
from jax import lax
from jax.sharding import PartitionSpec as P

BY = 4
MOST = 2
BZ = 64


def ring_pairs(axis):
    count = lax.axis_size(axis)
    forward = [(i, (i + 1) % count) for i in range(count)]
    backward = [(target, source) for source, target in forward]
    return forward, backward


def with_halo(block):
    x_forward, x_backward = ring_pairs("base")
    y_forward, y_backward = ring_pairs("fine")
    low_x = lax.ppermute(block[:, -1:], "base", x_forward)
    high_x = lax.ppermute(block[:, :1], "base", x_backward)
    low_y = lax.ppermute(block[:, :, -1:], "fine", y_forward)
    high_y = lax.ppermute(block[:, :, :1], "fine", y_backward)
    corner = jnp.zeros_like(block[:, :1, :1])
    low_y = jnp.concatenate([corner, low_y, corner], axis=1)
    high_y = jnp.concatenate([corner, high_y, corner], axis=1)
    block = jnp.concatenate([low_x, block, high_x], axis=1)
    return jnp.concatenate([low_y, block, high_y], axis=2)


def reaction(values, reaction_rates, left_ids, right_ids):
    fields = values.shape[0]
    levels = lax.broadcasted_iota(jnp.int32, (fields, fields), 1)
    pick_left = (left_ids[:, None] == levels).astype(jnp.float32)
    pick_right = (right_ids[:, None] == levels).astype(jnp.float32)
    left_term = jnp.einsum("fg,gxyz->fxyz", pick_left, values, precision=lax.Precision.HIGHEST)
    right_term = jnp.einsum("fg,gxyz->fxyz", pick_right, values, precision=lax.Precision.HIGHEST)
    return reaction_rates[:, None, None, None] * left_term * right_term


def coarse_advance(centre, neighbours, viscosity, reaction_rates, left_ids, right_ids):
    return (
        centre
        + viscosity[:, None, None, None] * (neighbours - 6.0 * centre)
        + reaction(centre, reaction_rates, left_ids, right_ids)
    )


def widen_face(face):
    return jnp.repeat(jnp.repeat(face, 2, axis=-2), 2, axis=-1)


def fine_advance(fine_box, faces, viscosity, reaction_rates, left_ids, right_ids):
    low_x, high_x, low_y, high_y, low_z, high_z = faces
    low_x = low_x[:, None]
    high_x = high_x[:, None]
    low_y = low_y[:, :, None]
    high_y = high_y[:, :, None]
    low_z = low_z[:, :, :, None]
    high_z = high_z[:, :, :, None]
    pair_x = jnp.concatenate([low_x, fine_box[:, :-1]], axis=1) + jnp.concatenate(
        [fine_box[:, 1:], high_x], axis=1
    )
    pair_y = jnp.concatenate([low_y, fine_box[:, :, :-1]], axis=2) + jnp.concatenate(
        [fine_box[:, :, 1:], high_y], axis=2
    )
    cells_z = fine_box.shape[3]
    z_pos = lax.broadcasted_iota(jnp.int32, fine_box.shape, 3)
    below = jnp.where(z_pos == 0, low_z, jnp.roll(fine_box, 1, 3))
    above = jnp.where(z_pos == cells_z - 1, high_z, jnp.roll(fine_box, -1, 3))
    pair_z = below + above
    neighbours = pair_x + pair_y + pair_z
    return (
        fine_box
        + 2.0 * viscosity[:, None, None, None] * (neighbours - 6.0 * fine_box)
        + 0.5 * reaction(fine_box, reaction_rates, left_ids, right_ids)
    )


def coarsen(fine_box):
    fields, cells_x, cells_y, cells_z = fine_box.shape
    pairs_x = fine_box.reshape(fields, cells_x // 2, 2, cells_y, cells_z).sum(axis=2)
    pairs_y = pairs_x.reshape(fields, cells_x // 2, cells_y // 2, 2, cells_z).sum(axis=3)
    pair_z = (
        lax.broadcasted_iota(jnp.int32, (cells_z, cells_z // 2), 0) // 2
        == lax.broadcasted_iota(jnp.int32, (cells_z, cells_z // 2), 1)
    ).astype(jnp.float32)
    summed = jnp.einsum("fxyz,zw->fxyw", pairs_y, pair_z, precision=lax.Precision.HIGHEST)
    return 0.125 * summed


def packed_faces(extended, offset, z_start):
    fields, rows_x, _, cells_z = extended.shape
    window = lax.dynamic_slice(extended, (0, 0, offset, 0), (fields, rows_x, BY + 2, cells_z))
    half = lax.dynamic_slice_in_dim(window, z_start, BZ, axis=3)
    low_x = half[:, 0, 1:-1, :]
    high_x = half[:, -1, 1:-1, :]
    low_y = half[:, 1:-1, 0, :]
    high_y = half[:, 1:-1, -1, :]
    inner = window[:, 1:-1, 1:-1, :]
    low_z = lax.dynamic_index_in_dim(inner, (z_start - 1) % cells_z, 3, keepdims=False)
    high_z = lax.dynamic_index_in_dim(inner, (z_start + BZ) % cells_z, 3, keepdims=False)
    return jnp.concatenate(
        [
            face_part.reshape(fields, -1)
            for face_part in (low_x, high_x, low_y, high_y, low_z, high_z)
        ],
        axis=1,
    )


def unpack_faces(packed, cells_x):
    pairs, fields = packed.shape[:2]
    widths = [BY * BZ, BY * BZ, cells_x * BZ, cells_x * BZ, cells_x * BY, cells_x * BY]
    shapes = [(BY, BZ), (BY, BZ), (cells_x, BZ), (cells_x, BZ), (cells_x, BY), (cells_x, BY)]
    face_list = []
    offset = 0
    for width_now, shape_now in zip(widths, shapes):
        part = packed[:, :, offset : offset + width_now].reshape((pairs, fields) + shape_now)
        face_list.append(widen_face(part))
        offset = offset + width_now
    return face_list


def per_device(
    coarse_level, fine_level, box_list, patch_owner, reaction_table, viscosity, reaction_rates
):
    fields, cells_x, height, cells_z = coarse_level.shape
    devices_fine = lax.axis_size("fine")
    my_index = lax.axis_index("fine")
    left_ids = reaction_table[:, 0]
    right_ids = reaction_table[:, 1]

    corners = box_list[0]
    owners = patch_owner[0]
    y_cell = corners[:, 0]
    z_cell = corners[:, 1]
    y_block = y_cell // height
    row_ids = lax.broadcasted_iota(jnp.int32, (devices_fine, devices_fine), 0)
    col_ids = lax.broadcasted_iota(jnp.int32, (devices_fine, devices_fine), 1)
    holder = jnp.sum(jnp.where(owners[None, :] == row_ids, col_ids, 0), axis=1)
    slot_rank = jnp.sum(
        jnp.where((y_block[:, None] == y_block[None, :]) & (col_ids < row_ids), 1, 0), axis=1
    )
    patch_ids = jnp.arange(devices_fine, dtype=jnp.int32)
    slot_patch = []
    slot_filled = []
    for slot_number in range(MOST):
        is_hit = (y_block == my_index) & (slot_rank == slot_number)
        slot_patch.append(jnp.sum(jnp.where(is_hit, patch_ids, 0)))
        slot_filled.append(jnp.any(is_hit))
    box_of_dest = holder
    dest_here = y_block[box_of_dest] == my_index
    dest_slot = slot_rank[box_of_dest]
    source_of_mine = y_block[holder[my_index]]

    def slot_faces(extended, slot_number):
        patch_id = slot_patch[slot_number]
        return packed_faces(extended, y_cell[patch_id] - my_index * height, z_cell[patch_id])

    old_ext = with_halo(coarse_level)
    centre = old_ext[:, 1:-1, 1:-1, :]
    neighbours = (
        old_ext[:, :-2, 1:-1, :]
        + old_ext[:, 2:, 1:-1, :]
        + (old_ext[:, 1:-1, :-2, :] + old_ext[:, 1:-1, 2:, :])
        + (jnp.roll(centre, 1, 3) + jnp.roll(centre, -1, 3))
    )
    coarse_next = coarse_advance(centre, neighbours, viscosity, reaction_rates, left_ids, right_ids)
    new_ext = with_halo(coarse_next)
    slots = [
        jnp.stack([slot_faces(old_ext, slot_number), slot_faces(new_ext, slot_number)])
        for slot_number in range(MOST)
    ]
    rows = jnp.where(
        (dest_here & (dest_slot == 0))[:, None],
        slots[0].reshape(1, -1),
        jnp.where(dest_here[:, None], slots[1].reshape(1, -1), 0.0),
    )
    arrived = lax.all_to_all(rows, "fine", 0, 0, tiled=True)
    shell_pair = lax.dynamic_index_in_dim(arrived, source_of_mine, 0, keepdims=False)
    shell_pair = shell_pair.reshape(slots[0].shape)
    wide_pair = unpack_faces(shell_pair, cells_x)
    old_faces = [wide[0] for wide in wide_pair]
    mid_faces = [0.5 * (wide[0] + wide[1]) for wide in wide_pair]

    fine_box = fine_level[0, 0]
    fine_box = fine_advance(fine_box, old_faces, viscosity, reaction_rates, left_ids, right_ids)
    fine_box = fine_advance(fine_box, mid_faces, viscosity, reaction_rates, left_ids, right_ids)
    averaged = coarsen(fine_box)

    dest_ids = lax.broadcasted_iota(jnp.int32, (devices_fine, 1), 0)
    sent = jnp.where(dest_ids == source_of_mine, averaged.reshape(1, -1), 0.0)
    rows_in = lax.all_to_all(sent, "fine", 0, 0, tiled=True)
    y_ids = lax.broadcasted_iota(jnp.int32, (height, cells_z), 0)
    z_ids = lax.broadcasted_iota(jnp.int32, (height, cells_z), 1)
    coarse_out = coarse_next
    for slot_number in range(MOST):
        patch_id = slot_patch[slot_number]
        offset = y_cell[patch_id] - my_index * height
        z_start = z_cell[patch_id]
        incoming = lax.dynamic_index_in_dim(rows_in, owners[patch_id], 0, keepdims=False)
        incoming = incoming.reshape(averaged.shape)
        tiled = jnp.tile(incoming, (1, 1, height // BY, cells_z // BZ))
        covered = (
            slot_filled[slot_number]
            & (y_ids >= offset)
            & (y_ids < offset + BY)
            & (z_ids >= z_start)
            & (z_ids < z_start + BZ)
        )
        coarse_out = jnp.where(covered[None, None], tiled, coarse_out)
    return (coarse_out, fine_box[None, None])


def solution(mesh):
    placed = (
        P(None, "base", "fine", None),
        P("base", "fine", None, None, None, None),
        P("base", None, None),
        P("base", None),
        P(),
        P(),
        P(),
    )
    return jax.shard_map(
        per_device,
        mesh=mesh,
        in_specs=placed,
        out_specs=(P(None, "base", "fine", None), P("base", "fine", None, None, None, None)),
        check_vma=False,
    )
```

```python
import jax
import jax.numpy as jnp
from jax import lax
from jax.sharding import PartitionSpec as P

BY = 4
MOST = 2
BZ = 64


def ring_pairs(axis):
    count = lax.axis_size(axis)
    forward = [(i, (i + 1) % count) for i in range(count)]
    backward = [(target, source) for source, target in forward]
    return forward, backward


def with_halo(block):
    x_forward, x_backward = ring_pairs("base")
    y_forward, y_backward = ring_pairs("fine")
    low_x = lax.ppermute(block[:, -1:], "base", x_forward)
    high_x = lax.ppermute(block[:, :1], "base", x_backward)
    low_y = lax.ppermute(block[:, :, -1:], "fine", y_forward)
    high_y = lax.ppermute(block[:, :, :1], "fine", y_backward)
    corner = jnp.zeros_like(block[:, :1, :1])
    low_y = jnp.concatenate([corner, low_y, corner], axis=1)
    high_y = jnp.concatenate([corner, high_y, corner], axis=1)
    block = jnp.concatenate([low_x, block, high_x], axis=1)
    return jnp.concatenate([low_y, block, high_y], axis=2)


def reaction(values, reaction_rates, left_ids, right_ids):
    fields = values.shape[0]
    levels = lax.broadcasted_iota(jnp.int32, (fields, fields), 1)
    pick_left = (left_ids[:, None] == levels).astype(jnp.float32)
    pick_right = (right_ids[:, None] == levels).astype(jnp.float32)
    left_term = jnp.einsum("fg,gxyz->fxyz", pick_left, values, precision=lax.Precision.HIGH)
    right_term = jnp.einsum("fg,gxyz->fxyz", pick_right, values, precision=lax.Precision.HIGH)
    return reaction_rates[:, None, None, None] * left_term * right_term


def coarse_advance(centre, neighbours, viscosity, reaction_rates, left_ids, right_ids):
    return (
        centre
        + viscosity[:, None, None, None] * (neighbours - 6.0 * centre)
        + reaction(centre, reaction_rates, left_ids, right_ids)
    )


def widen_face(face):
    return jnp.repeat(jnp.repeat(face, 2, axis=-2), 2, axis=-1)


def fine_advance(fine_box, faces, viscosity, reaction_rates, left_ids, right_ids):
    low_x, high_x, low_y, high_y, low_z, high_z = faces
    low_x = low_x[:, None]
    high_x = high_x[:, None]
    low_y = low_y[:, :, None]
    high_y = high_y[:, :, None]
    low_z = low_z[:, :, :, None]
    high_z = high_z[:, :, :, None]
    pair_x = jnp.concatenate([low_x, fine_box[:, :-1]], axis=1) + jnp.concatenate(
        [fine_box[:, 1:], high_x], axis=1
    )
    pair_y = jnp.concatenate([low_y, fine_box[:, :, :-1]], axis=2) + jnp.concatenate(
        [fine_box[:, :, 1:], high_y], axis=2
    )
    cells_z = fine_box.shape[3]
    z_pos = lax.broadcasted_iota(jnp.int32, fine_box.shape, 3)
    below = jnp.where(z_pos == 0, low_z, jnp.roll(fine_box, 1, 3))
    above = jnp.where(z_pos == cells_z - 1, high_z, jnp.roll(fine_box, -1, 3))
    pair_z = below + above
    neighbours = pair_x + pair_y + pair_z
    return (
        fine_box
        + 2.0 * viscosity[:, None, None, None] * (neighbours - 6.0 * fine_box)
        + 0.5 * reaction(fine_box, reaction_rates, left_ids, right_ids)
    )


def coarsen(fine_box):
    fields, cells_x, cells_y, cells_z = fine_box.shape
    pairs_x = fine_box.reshape(fields, cells_x // 2, 2, cells_y, cells_z).sum(axis=2)
    pairs_y = pairs_x.reshape(fields, cells_x // 2, cells_y // 2, 2, cells_z).sum(axis=3)
    pair_z = (
        lax.broadcasted_iota(jnp.int32, (cells_z, cells_z // 2), 0) // 2
        == lax.broadcasted_iota(jnp.int32, (cells_z, cells_z // 2), 1)
    ).astype(jnp.float32)
    summed = jnp.einsum("fxyz,zw->fxyw", pairs_y, pair_z, precision=lax.Precision.HIGHEST)
    return 0.125 * summed


def packed_faces(extended, offset, z_start):
    fields, rows_x, _, cells_z = extended.shape
    window = lax.dynamic_slice(extended, (0, 0, offset, 0), (fields, rows_x, BY + 2, cells_z))
    half = lax.dynamic_slice_in_dim(window, z_start, BZ, axis=3)
    low_x = half[:, 0, 1:-1, :]
    high_x = half[:, -1, 1:-1, :]
    low_y = half[:, 1:-1, 0, :]
    high_y = half[:, 1:-1, -1, :]
    inner = window[:, 1:-1, 1:-1, :]
    low_z = lax.dynamic_index_in_dim(inner, (z_start - 1) % cells_z, 3, keepdims=False)
    high_z = lax.dynamic_index_in_dim(inner, (z_start + BZ) % cells_z, 3, keepdims=False)
    return jnp.concatenate(
        [
            face_part.reshape(fields, -1)
            for face_part in (low_x, high_x, low_y, high_y, low_z, high_z)
        ],
        axis=1,
    )


def unpack_faces(packed, cells_x):
    pairs, fields = packed.shape[:2]
    widths = [BY * BZ, BY * BZ, cells_x * BZ, cells_x * BZ, cells_x * BY, cells_x * BY]
    shapes = [(BY, BZ), (BY, BZ), (cells_x, BZ), (cells_x, BZ), (cells_x, BY), (cells_x, BY)]
    face_list = []
    offset = 0
    for width_now, shape_now in zip(widths, shapes):
        part = packed[:, :, offset : offset + width_now].reshape((pairs, fields) + shape_now)
        face_list.append(widen_face(part))
        offset = offset + width_now
    return face_list


def per_device(
    coarse_level, fine_level, box_list, patch_owner, reaction_table, viscosity, reaction_rates
):
    fields, cells_x, height, cells_z = coarse_level.shape
    devices_fine = lax.axis_size("fine")
    my_index = lax.axis_index("fine")
    left_ids = reaction_table[:, 0]
    right_ids = reaction_table[:, 1]

    corners = box_list[0]
    owners = patch_owner[0]
    y_cell = corners[:, 0]
    z_cell = corners[:, 1]
    y_block = y_cell // height
    row_ids = lax.broadcasted_iota(jnp.int32, (devices_fine, devices_fine), 0)
    col_ids = lax.broadcasted_iota(jnp.int32, (devices_fine, devices_fine), 1)
    holder = jnp.sum(jnp.where(owners[None, :] == row_ids, col_ids, 0), axis=1)
    slot_rank = jnp.sum(
        jnp.where((y_block[:, None] == y_block[None, :]) & (col_ids < row_ids), 1, 0), axis=1
    )
    patch_ids = jnp.arange(devices_fine, dtype=jnp.int32)
    slot_patch = []
    slot_filled = []
    for slot_number in range(MOST):
        is_hit = (y_block == my_index) & (slot_rank == slot_number)
        slot_patch.append(jnp.sum(jnp.where(is_hit, patch_ids, 0)))
        slot_filled.append(jnp.any(is_hit))
    box_of_dest = holder
    dest_here = y_block[box_of_dest] == my_index
    dest_slot = slot_rank[box_of_dest]
    source_of_mine = y_block[holder[my_index]]

    def slot_faces(extended, slot_number):
        patch_id = slot_patch[slot_number]
        return packed_faces(extended, y_cell[patch_id] - my_index * height, z_cell[patch_id])

    old_ext = with_halo(coarse_level)
    centre = old_ext[:, 1:-1, 1:-1, :]
    neighbours = (
        old_ext[:, :-2, 1:-1, :]
        + old_ext[:, 2:, 1:-1, :]
        + (old_ext[:, 1:-1, :-2, :] + old_ext[:, 1:-1, 2:, :])
        + (jnp.roll(centre, 1, 3) + jnp.roll(centre, -1, 3))
    )
    coarse_next = coarse_advance(centre, neighbours, viscosity, reaction_rates, left_ids, right_ids)
    new_ext = with_halo(coarse_next)
    slots = [
        jnp.stack([slot_faces(old_ext, slot_number), slot_faces(new_ext, slot_number)])
        for slot_number in range(MOST)
    ]
    rows = jnp.where(
        (dest_here & (dest_slot == 0))[:, None],
        slots[0].reshape(1, -1),
        jnp.where(dest_here[:, None], slots[1].reshape(1, -1), 0.0),
    )
    arrived = lax.all_to_all(rows, "fine", 0, 0, tiled=True)
    shell_pair = lax.dynamic_index_in_dim(arrived, source_of_mine, 0, keepdims=False)
    shell_pair = shell_pair.reshape(slots[0].shape)
    wide_pair = unpack_faces(shell_pair, cells_x)
    old_faces = [wide[0] for wide in wide_pair]
    mid_faces = [0.5 * (wide[0] + wide[1]) for wide in wide_pair]

    fine_box = fine_level[0, 0]
    fine_box = fine_advance(fine_box, old_faces, viscosity, reaction_rates, left_ids, right_ids)
    fine_box = fine_advance(fine_box, mid_faces, viscosity, reaction_rates, left_ids, right_ids)
    averaged = coarsen(fine_box)

    dest_ids = lax.broadcasted_iota(jnp.int32, (devices_fine, 1), 0)
    sent = jnp.where(dest_ids == source_of_mine, averaged.reshape(1, -1), 0.0)
    rows_in = lax.all_to_all(sent, "fine", 0, 0, tiled=True)
    y_ids = lax.broadcasted_iota(jnp.int32, (height, cells_z), 0)
    z_ids = lax.broadcasted_iota(jnp.int32, (height, cells_z), 1)
    coarse_out = coarse_next
    for slot_number in range(MOST):
        patch_id = slot_patch[slot_number]
        offset = y_cell[patch_id] - my_index * height
        z_start = z_cell[patch_id]
        incoming = lax.dynamic_index_in_dim(rows_in, owners[patch_id], 0, keepdims=False)
        incoming = incoming.reshape(averaged.shape)
        tiled = jnp.tile(incoming, (1, 1, height // BY, cells_z // BZ))
        covered = (
            slot_filled[slot_number]
            & (y_ids >= offset)
            & (y_ids < offset + BY)
            & (z_ids >= z_start)
            & (z_ids < z_start + BZ)
        )
        coarse_out = jnp.where(covered[None, None], tiled, coarse_out)
    return (coarse_out, fine_box[None, None])


def solution(mesh):
    placed = (
        P(None, "base", "fine", None),
        P("base", "fine", None, None, None, None),
        P("base", None, None),
        P("base", None),
        P(),
        P(),
        P(),
    )
    return jax.shard_map(
        per_device,
        mesh=mesh,
        in_specs=placed,
        out_specs=(P(None, "base", "fine", None), P("base", "fine", None, None, None, None)),
        check_vma=False,
    )
```

```python
import jax
import jax.numpy as jnp
from jax import lax
from jax.sharding import PartitionSpec as P

BY = 4
MOST = 2
BZ = 64


def ring_pairs(axis):
    count = lax.axis_size(axis)
    forward = [(i, (i + 1) % count) for i in range(count)]
    backward = [(target, source) for source, target in forward]
    return forward, backward


def with_halo(block):
    x_forward, x_backward = ring_pairs("base")
    y_forward, y_backward = ring_pairs("fine")
    low_x = lax.ppermute(block[:, -1:], "base", x_forward)
    high_x = lax.ppermute(block[:, :1], "base", x_backward)
    low_y = lax.ppermute(block[:, :, -1:], "fine", y_forward)
    high_y = lax.ppermute(block[:, :, :1], "fine", y_backward)
    corner = jnp.zeros_like(block[:, :1, :1])
    low_y = jnp.concatenate([corner, low_y, corner], axis=1)
    high_y = jnp.concatenate([corner, high_y, corner], axis=1)
    block = jnp.concatenate([low_x, block, high_x], axis=1)
    return jnp.concatenate([low_y, block, high_y], axis=2)


def reaction(values, reaction_rates, left_ids, right_ids):
    fields = values.shape[0]
    levels = lax.broadcasted_iota(jnp.int32, (fields, fields), 1)
    pick_left = (left_ids[:, None] == levels).astype(jnp.float32)
    pick_right = (right_ids[:, None] == levels).astype(jnp.float32)
    left_term = jnp.einsum("fg,gxyz->fxyz", pick_left, values, precision=lax.Precision.HIGHEST)
    right_term = jnp.einsum("fg,gxyz->fxyz", pick_right, values, precision=lax.Precision.HIGHEST)
    return reaction_rates[:, None, None, None] * left_term * right_term


def coarse_advance(centre, neighbours, viscosity, reaction_rates, left_ids, right_ids):
    return (
        centre
        + viscosity[:, None, None, None] * (neighbours - 6.0 * centre)
        + reaction(centre, reaction_rates, left_ids, right_ids)
    )


def widen_face(face):
    return jnp.repeat(jnp.repeat(face, 2, axis=-2), 2, axis=-1)


def fine_advance(fine_box, faces, viscosity, reaction_rates, left_ids, right_ids):
    low_x, high_x, low_y, high_y, low_z, high_z = faces
    low_x = low_x[:, None]
    high_x = high_x[:, None]
    low_y = low_y[:, :, None]
    high_y = high_y[:, :, None]
    low_z = low_z[:, :, :, None]
    high_z = high_z[:, :, :, None]
    pair_x = jnp.concatenate([low_x, fine_box[:, :-1]], axis=1) + jnp.concatenate(
        [fine_box[:, 1:], high_x], axis=1
    )
    pair_y = jnp.concatenate([low_y, fine_box[:, :, :-1]], axis=2) + jnp.concatenate(
        [fine_box[:, :, 1:], high_y], axis=2
    )
    cells_z = fine_box.shape[3]
    z_pos = lax.broadcasted_iota(jnp.int32, fine_box.shape, 3)
    below = jnp.where(z_pos == 0, low_z, jnp.roll(fine_box, 1, 3))
    above = jnp.where(z_pos == cells_z - 1, high_z, jnp.roll(fine_box, -1, 3))
    pair_z = below + above
    neighbours = pair_x + pair_y + pair_z
    return (
        fine_box
        + 2.0 * viscosity[:, None, None, None] * (neighbours - 6.0 * fine_box)
        + 0.5 * reaction(fine_box, reaction_rates, left_ids, right_ids)
    )


def face_terms(faces, shape):
    low_x, high_x, low_y, high_y, low_z, high_z = faces
    fields, cells_x, cells_y, cells_z = shape
    along_x = jnp.concatenate(
        [low_x[:, None], jnp.zeros((fields, cells_x - 2, cells_y, cells_z)), high_x[:, None]],
        axis=1,
    )
    along_y = jnp.concatenate(
        [
            low_y[:, :, None],
            jnp.zeros((fields, cells_x, cells_y - 2, cells_z)),
            high_y[:, :, None],
        ],
        axis=2,
    )
    along_z = jnp.concatenate(
        [
            low_z[:, :, :, None],
            jnp.zeros((fields, cells_x, cells_y, cells_z - 2)),
            high_z[:, :, :, None],
        ],
        axis=3,
    )
    return along_x + along_y + along_z


def coarsen(fine_box):
    fields, cells_x, cells_y, cells_z = fine_box.shape
    pairs_x = fine_box.reshape(fields, cells_x // 2, 2, cells_y, cells_z).sum(axis=2)
    pairs_y = pairs_x.reshape(fields, cells_x // 2, cells_y // 2, 2, cells_z).sum(axis=3)
    pair_z = (
        lax.broadcasted_iota(jnp.int32, (cells_z, cells_z // 2), 0) // 2
        == lax.broadcasted_iota(jnp.int32, (cells_z, cells_z // 2), 1)
    ).astype(jnp.float32)
    summed = jnp.einsum("fxyz,zw->fxyw", pairs_y, pair_z, precision=lax.Precision.HIGHEST)
    return 0.125 * summed


def packed_faces(extended, offset, z_start):
    fields, rows_x, _, cells_z = extended.shape
    window = lax.dynamic_slice(extended, (0, 0, offset, 0), (fields, rows_x, BY + 2, cells_z))
    half = lax.dynamic_slice_in_dim(window, z_start, BZ, axis=3)
    low_x = half[:, 0, 1:-1, :]
    high_x = half[:, -1, 1:-1, :]
    low_y = half[:, 1:-1, 0, :]
    high_y = half[:, 1:-1, -1, :]
    inner = window[:, 1:-1, 1:-1, :]
    low_z = lax.dynamic_index_in_dim(inner, (z_start - 1) % cells_z, 3, keepdims=False)
    high_z = lax.dynamic_index_in_dim(inner, (z_start + BZ) % cells_z, 3, keepdims=False)
    return jnp.concatenate(
        [
            face_part.reshape(fields, -1)
            for face_part in (low_x, high_x, low_y, high_y, low_z, high_z)
        ],
        axis=1,
    )


def unpack_faces(packed, cells_x):
    pairs, fields = packed.shape[:2]
    widths = [BY * BZ, BY * BZ, cells_x * BZ, cells_x * BZ, cells_x * BY, cells_x * BY]
    shapes = [(BY, BZ), (BY, BZ), (cells_x, BZ), (cells_x, BZ), (cells_x, BY), (cells_x, BY)]
    face_list = []
    offset = 0
    for width_now, shape_now in zip(widths, shapes):
        part = packed[:, :, offset : offset + width_now].reshape((pairs, fields) + shape_now)
        face_list.append(widen_face(part))
        offset = offset + width_now
    return face_list


def per_device(
    coarse_level, fine_level, box_list, patch_owner, reaction_table, viscosity, reaction_rates
):
    fields, cells_x, height, cells_z = coarse_level.shape
    devices_fine = lax.axis_size("fine")
    my_index = lax.axis_index("fine")
    left_ids = reaction_table[:, 0]
    right_ids = reaction_table[:, 1]

    corners = box_list[0]
    owners = patch_owner[0]
    y_cell = corners[:, 0]
    z_cell = corners[:, 1]
    y_block = y_cell // height
    row_ids = lax.broadcasted_iota(jnp.int32, (devices_fine, devices_fine), 0)
    col_ids = lax.broadcasted_iota(jnp.int32, (devices_fine, devices_fine), 1)
    holder = jnp.sum(jnp.where(owners[None, :] == row_ids, col_ids, 0), axis=1)
    slot_rank = jnp.sum(
        jnp.where((y_block[:, None] == y_block[None, :]) & (col_ids < row_ids), 1, 0), axis=1
    )
    patch_ids = jnp.arange(devices_fine, dtype=jnp.int32)
    slot_patch = []
    slot_filled = []
    for slot_number in range(MOST):
        is_hit = (y_block == my_index) & (slot_rank == slot_number)
        slot_patch.append(jnp.sum(jnp.where(is_hit, patch_ids, 0)))
        slot_filled.append(jnp.any(is_hit))
    box_of_dest = holder
    dest_here = y_block[box_of_dest] == my_index
    dest_slot = slot_rank[box_of_dest]
    source_of_mine = y_block[holder[my_index]]

    def slot_faces(extended, slot_number):
        patch_id = slot_patch[slot_number]
        return packed_faces(extended, y_cell[patch_id] - my_index * height, z_cell[patch_id])

    old_ext = with_halo(coarse_level)
    centre = old_ext[:, 1:-1, 1:-1, :]
    neighbours = (
        old_ext[:, :-2, 1:-1, :]
        + old_ext[:, 2:, 1:-1, :]
        + (old_ext[:, 1:-1, :-2, :] + old_ext[:, 1:-1, 2:, :])
        + (jnp.roll(centre, 1, 3) + jnp.roll(centre, -1, 3))
    )
    coarse_next = coarse_advance(centre, neighbours, viscosity, reaction_rates, left_ids, right_ids)
    new_ext = with_halo(coarse_next)
    slots = [
        jnp.stack([slot_faces(old_ext, slot_number), slot_faces(new_ext, slot_number)])
        for slot_number in range(MOST)
    ]
    rows = jnp.where(
        (dest_here & (dest_slot == 0))[:, None],
        slots[0].reshape(1, -1),
        jnp.where(dest_here[:, None], slots[1].reshape(1, -1), 0.0),
    )
    arrived = lax.all_to_all(rows, "fine", 0, 0, tiled=True)
    shell_pair = lax.dynamic_index_in_dim(arrived, source_of_mine, 0, keepdims=False)
    shell_pair = shell_pair.reshape(slots[0].shape)
    wide_pair = unpack_faces(shell_pair, cells_x)
    old_faces = [wide[0] for wide in wide_pair]
    mid_faces = [0.5 * (wide[0] + wide[1]) for wide in wide_pair]

    fine_box = fine_level[0, 0]
    open_faces = [jnp.zeros_like(wide) for wide in old_faces]
    fine_box = fine_advance(fine_box, open_faces, viscosity, reaction_rates, left_ids, right_ids)
    fine_box = lax.optimization_barrier(fine_box)
    fine_box = fine_box + 2.0 * viscosity[:, None, None, None] * face_terms(
        old_faces, fine_box.shape
    )
    fine_box = fine_advance(fine_box, mid_faces, viscosity, reaction_rates, left_ids, right_ids)
    averaged = coarsen(fine_box)

    dest_ids = lax.broadcasted_iota(jnp.int32, (devices_fine, 1), 0)
    sent = jnp.where(dest_ids == source_of_mine, averaged.reshape(1, -1), 0.0)
    rows_in = lax.all_to_all(sent, "fine", 0, 0, tiled=True)
    y_ids = lax.broadcasted_iota(jnp.int32, (height, cells_z), 0)
    z_ids = lax.broadcasted_iota(jnp.int32, (height, cells_z), 1)
    coarse_out = coarse_next
    for slot_number in range(MOST):
        patch_id = slot_patch[slot_number]
        offset = y_cell[patch_id] - my_index * height
        z_start = z_cell[patch_id]
        incoming = lax.dynamic_index_in_dim(rows_in, owners[patch_id], 0, keepdims=False)
        incoming = incoming.reshape(averaged.shape)
        tiled = jnp.tile(incoming, (1, 1, height // BY, cells_z // BZ))
        covered = (
            slot_filled[slot_number]
            & (y_ids >= offset)
            & (y_ids < offset + BY)
            & (z_ids >= z_start)
            & (z_ids < z_start + BZ)
        )
        coarse_out = jnp.where(covered[None, None], tiled, coarse_out)
    return (coarse_out, fine_box[None, None])


def solution(mesh):
    placed = (
        P(None, "base", "fine", None),
        P("base", "fine", None, None, None, None),
        P("base", None, None),
        P("base", None),
        P(),
        P(),
        P(),
    )
    return jax.shard_map(
        per_device,
        mesh=mesh,
        in_specs=placed,
        out_specs=(P(None, "base", "fine", None), P("base", "fine", None, None, None, None)),
        check_vma=False,
    )
```

```python
import jax
import jax.numpy as jnp
from jax import lax
from jax.sharding import PartitionSpec as P

BY = 4
MOST = 2
BZ = 64


def ring_pairs(axis):
    count = lax.axis_size(axis)
    forward = [(i, (i + 1) % count) for i in range(count)]
    backward = [(target, source) for source, target in forward]
    return forward, backward


def with_halo(block):
    x_forward, x_backward = ring_pairs("base")
    y_forward, y_backward = ring_pairs("fine")
    low_x = lax.ppermute(block[:, -1:], "base", x_forward)
    high_x = lax.ppermute(block[:, :1], "base", x_backward)
    low_y = lax.ppermute(block[:, :, -1:], "fine", y_forward)
    high_y = lax.ppermute(block[:, :, :1], "fine", y_backward)
    corner = jnp.zeros_like(block[:, :1, :1])
    low_y = jnp.concatenate([corner, low_y, corner], axis=1)
    high_y = jnp.concatenate([corner, high_y, corner], axis=1)
    block = jnp.concatenate([low_x, block, high_x], axis=1)
    return jnp.concatenate([low_y, block, high_y], axis=2)


def reaction(values, reaction_rates, left_ids, right_ids):
    fields = values.shape[0]
    levels = lax.broadcasted_iota(jnp.int32, (fields, fields), 1)
    pick_left = (left_ids[:, None] == levels).astype(jnp.float32)
    pick_right = (right_ids[:, None] == levels).astype(jnp.float32)
    left_term = jnp.einsum("fg,gxyz->fxyz", pick_left, values, precision=lax.Precision.HIGHEST)
    right_term = jnp.einsum("fg,gxyz->fxyz", pick_right, values, precision=lax.Precision.HIGHEST)
    return reaction_rates[:, None, None, None] * left_term * right_term


def coarse_advance(centre, neighbours, viscosity, reaction_rates, left_ids, right_ids):
    return (
        centre
        + viscosity[:, None, None, None] * (neighbours - 6.0 * centre)
        + reaction(centre, reaction_rates, left_ids, right_ids)
    )


def widen_face(face):
    return jnp.repeat(jnp.repeat(face, 2, axis=-2), 2, axis=-1)


def fine_advance(fine_box, faces, viscosity, reaction_rates, left_ids, right_ids):
    low_x, high_x, low_y, high_y, low_z, high_z = faces
    low_x = low_x[:, None]
    high_x = high_x[:, None]
    low_y = low_y[:, :, None]
    high_y = high_y[:, :, None]
    low_z = low_z[:, :, :, None]
    high_z = high_z[:, :, :, None]
    pair_x = jnp.concatenate([low_x, fine_box[:, :-1]], axis=1) + jnp.concatenate(
        [fine_box[:, 1:], high_x], axis=1
    )
    pair_y = jnp.concatenate([low_y, fine_box[:, :, :-1]], axis=2) + jnp.concatenate(
        [fine_box[:, :, 1:], high_y], axis=2
    )
    cells_z = fine_box.shape[3]
    z_pos = lax.broadcasted_iota(jnp.int32, fine_box.shape, 3)
    below = jnp.where(z_pos == 0, low_z, jnp.roll(fine_box, 1, 3))
    above = jnp.where(z_pos == cells_z - 1, high_z, jnp.roll(fine_box, -1, 3))
    pair_z = below + above
    neighbours = pair_x + pair_y + pair_z
    return (
        fine_box
        + 2.0 * viscosity[:, None, None, None] * (neighbours - 6.0 * fine_box)
        + 0.5 * reaction(fine_box, reaction_rates, left_ids, right_ids)
    )


def coarsen(fine_box):
    fields, cells_x, cells_y, cells_z = fine_box.shape
    pairs_x = fine_box.reshape(fields, cells_x // 2, 2, cells_y, cells_z).sum(axis=2)
    pairs_y = pairs_x.reshape(fields, cells_x // 2, cells_y // 2, 2, cells_z).sum(axis=3)
    pair_z = (
        lax.broadcasted_iota(jnp.int32, (cells_z, cells_z // 2), 0) // 2
        == lax.broadcasted_iota(jnp.int32, (cells_z, cells_z // 2), 1)
    ).astype(jnp.float32)
    summed = jnp.einsum("fxyz,zw->fxyw", pairs_y, pair_z, precision=lax.Precision.HIGHEST)
    return 0.125 * summed


def packed_faces(extended, offset, z_start):
    fields, rows_x, _, cells_z = extended.shape
    window = lax.dynamic_slice(extended, (0, 0, offset, 0), (fields, rows_x, BY + 2, cells_z))
    half = lax.dynamic_slice_in_dim(window, z_start, BZ, axis=3)
    low_x = half[:, 0, 1:-1, :]
    high_x = half[:, -1, 1:-1, :]
    low_y = half[:, 1:-1, 0, :]
    high_y = half[:, 1:-1, -1, :]
    inner = window[:, 1:-1, 1:-1, :]
    low_z = lax.dynamic_index_in_dim(inner, (z_start - 1) % cells_z, 3, keepdims=False)
    high_z = lax.dynamic_index_in_dim(inner, (z_start + BZ) % cells_z, 3, keepdims=False)
    return jnp.concatenate(
        [
            face_part.reshape(fields, -1)
            for face_part in (low_x, high_x, low_y, high_y, low_z, high_z)
        ],
        axis=1,
    )


def unpack_faces(packed, cells_x):
    pairs, fields = packed.shape[:2]
    widths = [BY * BZ, BY * BZ, cells_x * BZ, cells_x * BZ, cells_x * BY, cells_x * BY]
    shapes = [(BY, BZ), (BY, BZ), (cells_x, BZ), (cells_x, BZ), (cells_x, BY), (cells_x, BY)]
    face_list = []
    offset = 0
    for width_now, shape_now in zip(widths, shapes):
        part = packed[:, :, offset : offset + width_now].reshape((pairs, fields) + shape_now)
        face_list.append(widen_face(part))
        offset = offset + width_now
    return face_list


def per_device(
    coarse_level, fine_level, box_list, patch_owner, reaction_table, viscosity, reaction_rates
):
    fields, cells_x, height, cells_z = coarse_level.shape
    devices_fine = lax.axis_size("fine")
    my_index = lax.axis_index("fine")
    left_ids = reaction_table[:, 0]
    right_ids = reaction_table[:, 1]

    corners = box_list[0]
    owners = patch_owner[0]
    y_cell = corners[:, 0]
    z_cell = corners[:, 1]
    y_block = y_cell // height
    row_ids = lax.broadcasted_iota(jnp.int32, (devices_fine, devices_fine), 0)
    col_ids = lax.broadcasted_iota(jnp.int32, (devices_fine, devices_fine), 1)
    holder = jnp.sum(jnp.where(owners[None, :] == row_ids, col_ids, 0), axis=1)
    slot_rank = jnp.sum(
        jnp.where((y_block[:, None] == y_block[None, :]) & (col_ids < row_ids), 1, 0), axis=1
    )
    patch_ids = jnp.arange(devices_fine, dtype=jnp.int32)
    slot_patch = []
    slot_filled = []
    for slot_number in range(MOST):
        is_hit = (y_block == my_index) & (slot_rank == slot_number)
        slot_patch.append(jnp.sum(jnp.where(is_hit, patch_ids, 0)))
        slot_filled.append(jnp.any(is_hit))
    box_of_dest = holder
    dest_here = y_block[box_of_dest] == my_index
    dest_slot = slot_rank[box_of_dest]
    source_of_mine = y_block[holder[my_index]]

    def slot_faces(extended, slot_number):
        patch_id = slot_patch[slot_number]
        return packed_faces(extended, y_cell[patch_id] - my_index * height, z_cell[patch_id])

    old_ext = with_halo(coarse_level)
    centre = old_ext[:, 1:-1, 1:-1, :]
    neighbours = (
        old_ext[:, :-2, 1:-1, :]
        + old_ext[:, 2:, 1:-1, :]
        + (old_ext[:, 1:-1, :-2, :] + old_ext[:, 1:-1, 2:, :])
        + (jnp.roll(centre, 1, 3) + jnp.roll(centre, -1, 3))
    )
    coarse_next = coarse_advance(centre, neighbours, viscosity, reaction_rates, left_ids, right_ids)
    new_ext = with_halo(coarse_next)
    slots = [
        jnp.stack([slot_faces(old_ext, slot_number), slot_faces(new_ext, slot_number)])
        for slot_number in range(MOST)
    ]
    rows = jnp.where(
        (dest_here & (dest_slot == 0))[:, None],
        slots[0].reshape(1, -1),
        jnp.where(dest_here[:, None], slots[1].reshape(1, -1), 0.0),
    )
    arrived = lax.all_to_all(rows.reshape(devices_fine, -1, 128), "fine", 0, 0, tiled=True)
    shell_pair = lax.dynamic_index_in_dim(arrived, source_of_mine, 0, keepdims=False)
    shell_pair = shell_pair.reshape(slots[0].shape)
    wide_pair = unpack_faces(shell_pair, cells_x)
    old_faces = [wide[0] for wide in wide_pair]
    mid_faces = [0.5 * (wide[0] + wide[1]) for wide in wide_pair]

    fine_box = fine_level[0, 0]
    fine_box = fine_advance(fine_box, old_faces, viscosity, reaction_rates, left_ids, right_ids)
    fine_box = fine_advance(fine_box, mid_faces, viscosity, reaction_rates, left_ids, right_ids)
    averaged = coarsen(fine_box)

    dest_ids = lax.broadcasted_iota(jnp.int32, (devices_fine, 1), 0)
    sent = jnp.where(dest_ids == source_of_mine, averaged.reshape(1, -1), 0.0)
    rows_in = lax.all_to_all(sent.reshape(devices_fine, -1, 128), "fine", 0, 0, tiled=True)
    y_ids = lax.broadcasted_iota(jnp.int32, (height, cells_z), 0)
    z_ids = lax.broadcasted_iota(jnp.int32, (height, cells_z), 1)
    coarse_out = coarse_next
    for slot_number in range(MOST):
        patch_id = slot_patch[slot_number]
        offset = y_cell[patch_id] - my_index * height
        z_start = z_cell[patch_id]
        incoming = lax.dynamic_index_in_dim(rows_in, owners[patch_id], 0, keepdims=False)
        incoming = incoming.reshape(averaged.shape)
        tiled = jnp.tile(incoming, (1, 1, height // BY, cells_z // BZ))
        covered = (
            slot_filled[slot_number]
            & (y_ids >= offset)
            & (y_ids < offset + BY)
            & (z_ids >= z_start)
            & (z_ids < z_start + BZ)
        )
        coarse_out = jnp.where(covered[None, None], tiled, coarse_out)
    return (coarse_out, fine_box[None, None])


def solution(mesh):
    placed = (
        P(None, "base", "fine", None),
        P("base", "fine", None, None, None, None),
        P("base", None, None),
        P("base", None),
        P(),
        P(),
        P(),
    )
    return jax.shard_map(
        per_device,
        mesh=mesh,
        in_specs=placed,
        out_specs=(P(None, "base", "fine", None), P("base", "fine", None, None, None, None)),
        check_vma=False,
    )
```

```python
import jax
import jax.numpy as jnp
from jax import lax
from jax.sharding import PartitionSpec as P

BY = 4
MOST = 2
BZ = 64


def ring_pairs(axis):
    count = lax.axis_size(axis)
    forward = [(i, (i + 1) % count) for i in range(count)]
    backward = [(target, source) for source, target in forward]
    return forward, backward


def with_halo(block, edges=None):
    if edges is None:
        edges = (block[:, :1], block[:, -1:], block[:, :, :1], block[:, :, -1:])
    first_x, last_x, first_y, last_y = edges
    x_forward, x_backward = ring_pairs("base")
    y_forward, y_backward = ring_pairs("fine")
    low_x = lax.ppermute(last_x, "base", x_forward)
    high_x = lax.ppermute(first_x, "base", x_backward)
    low_y = lax.ppermute(last_y, "fine", y_forward)
    high_y = lax.ppermute(first_y, "fine", y_backward)
    corner = jnp.zeros_like(block[:, :1, :1])
    low_y = jnp.concatenate([corner, low_y, corner], axis=1)
    high_y = jnp.concatenate([corner, high_y, corner], axis=1)
    block = jnp.concatenate([low_x, block, high_x], axis=1)
    return jnp.concatenate([low_y, block, high_y], axis=2)


def reaction(values, reaction_rates, left_ids, right_ids):
    fields = values.shape[0]
    levels = lax.broadcasted_iota(jnp.int32, (fields, fields), 1)
    pick_left = (left_ids[:, None] == levels).astype(jnp.float32)
    pick_right = (right_ids[:, None] == levels).astype(jnp.float32)
    left_term = jnp.einsum("fg,gxyz->fxyz", pick_left, values, precision=lax.Precision.HIGHEST)
    right_term = jnp.einsum("fg,gxyz->fxyz", pick_right, values, precision=lax.Precision.HIGHEST)
    return reaction_rates[:, None, None, None] * left_term * right_term


def coarse_advance(centre, neighbours, viscosity, reaction_rates, left_ids, right_ids):
    return (
        centre
        + viscosity[:, None, None, None] * (neighbours - 6.0 * centre)
        + reaction(centre, reaction_rates, left_ids, right_ids)
    )


def widen_face(face):
    return jnp.repeat(jnp.repeat(face, 2, axis=-2), 2, axis=-1)


def fine_advance(fine_box, faces, viscosity, reaction_rates, left_ids, right_ids):
    low_x, high_x, low_y, high_y, low_z, high_z = faces
    low_x = low_x[:, None]
    high_x = high_x[:, None]
    low_y = low_y[:, :, None]
    high_y = high_y[:, :, None]
    low_z = low_z[:, :, :, None]
    high_z = high_z[:, :, :, None]
    pair_x = jnp.concatenate([low_x, fine_box[:, :-1]], axis=1) + jnp.concatenate(
        [fine_box[:, 1:], high_x], axis=1
    )
    pair_y = jnp.concatenate([low_y, fine_box[:, :, :-1]], axis=2) + jnp.concatenate(
        [fine_box[:, :, 1:], high_y], axis=2
    )
    cells_z = fine_box.shape[3]
    z_pos = lax.broadcasted_iota(jnp.int32, fine_box.shape, 3)
    below = jnp.where(z_pos == 0, low_z, jnp.roll(fine_box, 1, 3))
    above = jnp.where(z_pos == cells_z - 1, high_z, jnp.roll(fine_box, -1, 3))
    pair_z = below + above
    neighbours = pair_x + pair_y + pair_z
    return (
        fine_box
        + 2.0 * viscosity[:, None, None, None] * (neighbours - 6.0 * fine_box)
        + 0.5 * reaction(fine_box, reaction_rates, left_ids, right_ids)
    )


def coarsen(fine_box):
    fields, cells_x, cells_y, cells_z = fine_box.shape
    pairs_x = fine_box.reshape(fields, cells_x // 2, 2, cells_y, cells_z).sum(axis=2)
    pairs_y = pairs_x.reshape(fields, cells_x // 2, cells_y // 2, 2, cells_z).sum(axis=3)
    pair_z = (
        lax.broadcasted_iota(jnp.int32, (cells_z, cells_z // 2), 0) // 2
        == lax.broadcasted_iota(jnp.int32, (cells_z, cells_z // 2), 1)
    ).astype(jnp.float32)
    summed = jnp.einsum("fxyz,zw->fxyw", pairs_y, pair_z, precision=lax.Precision.HIGHEST)
    return 0.125 * summed


def packed_faces(extended, offset, z_start):
    fields, rows_x, _, cells_z = extended.shape
    window = lax.dynamic_slice(extended, (0, 0, offset, 0), (fields, rows_x, BY + 2, cells_z))
    half = lax.dynamic_slice_in_dim(window, z_start, BZ, axis=3)
    low_x = half[:, 0, 1:-1, :]
    high_x = half[:, -1, 1:-1, :]
    low_y = half[:, 1:-1, 0, :]
    high_y = half[:, 1:-1, -1, :]
    inner = window[:, 1:-1, 1:-1, :]
    low_z = lax.dynamic_index_in_dim(inner, (z_start - 1) % cells_z, 3, keepdims=False)
    high_z = lax.dynamic_index_in_dim(inner, (z_start + BZ) % cells_z, 3, keepdims=False)
    return jnp.concatenate(
        [
            face_part.reshape(fields, -1)
            for face_part in (low_x, high_x, low_y, high_y, low_z, high_z)
        ],
        axis=1,
    )


def unpack_faces(packed, cells_x):
    pairs, fields = packed.shape[:2]
    widths = [BY * BZ, BY * BZ, cells_x * BZ, cells_x * BZ, cells_x * BY, cells_x * BY]
    shapes = [(BY, BZ), (BY, BZ), (cells_x, BZ), (cells_x, BZ), (cells_x, BY), (cells_x, BY)]
    face_list = []
    offset = 0
    for width_now, shape_now in zip(widths, shapes):
        part = packed[:, :, offset : offset + width_now].reshape((pairs, fields) + shape_now)
        face_list.append(widen_face(part))
        offset = offset + width_now
    return face_list


def per_device(
    coarse_level, fine_level, box_list, patch_owner, reaction_table, viscosity, reaction_rates
):
    fields, cells_x, height, cells_z = coarse_level.shape
    devices_fine = lax.axis_size("fine")
    my_index = lax.axis_index("fine")
    left_ids = reaction_table[:, 0]
    right_ids = reaction_table[:, 1]

    corners = box_list[0]
    owners = patch_owner[0]
    y_cell = corners[:, 0]
    z_cell = corners[:, 1]
    y_block = y_cell // height
    row_ids = lax.broadcasted_iota(jnp.int32, (devices_fine, devices_fine), 0)
    col_ids = lax.broadcasted_iota(jnp.int32, (devices_fine, devices_fine), 1)
    holder = jnp.sum(jnp.where(owners[None, :] == row_ids, col_ids, 0), axis=1)
    slot_rank = jnp.sum(
        jnp.where((y_block[:, None] == y_block[None, :]) & (col_ids < row_ids), 1, 0), axis=1
    )
    patch_ids = jnp.arange(devices_fine, dtype=jnp.int32)
    slot_patch = []
    slot_filled = []
    for slot_number in range(MOST):
        is_hit = (y_block == my_index) & (slot_rank == slot_number)
        slot_patch.append(jnp.sum(jnp.where(is_hit, patch_ids, 0)))
        slot_filled.append(jnp.any(is_hit))
    box_of_dest = holder
    dest_here = y_block[box_of_dest] == my_index
    dest_slot = slot_rank[box_of_dest]
    source_of_mine = y_block[holder[my_index]]

    def slot_faces(extended, slot_number):
        patch_id = slot_patch[slot_number]
        return packed_faces(extended, y_cell[patch_id] - my_index * height, z_cell[patch_id])

    old_ext = with_halo(coarse_level)

    def advance_region(x0, x1, y0, y1):
        centre = old_ext[:, 1 + x0 : 1 + x1, 1 + y0 : 1 + y1, :]
        neighbours = (
            old_ext[:, x0:x1, 1 + y0 : 1 + y1, :]
            + old_ext[:, 2 + x0 : 2 + x1, 1 + y0 : 1 + y1, :]
            + (old_ext[:, 1 + x0 : 1 + x1, y0:y1, :] + old_ext[:, 1 + x0 : 1 + x1, 2 + y0 : 2 + y1, :])
            + (jnp.roll(centre, 1, 3) + jnp.roll(centre, -1, 3))
        )
        return coarse_advance(
            centre, neighbours, viscosity, reaction_rates, left_ids, right_ids
        )

    coarse_next = advance_region(0, cells_x, 0, height)
    edges = (
        advance_region(0, 1, 0, height),
        advance_region(cells_x - 1, cells_x, 0, height),
        advance_region(0, cells_x, 0, 1),
        advance_region(0, cells_x, height - 1, height),
    )
    new_ext = with_halo(coarse_next, edges)
    slots = [
        jnp.stack([slot_faces(old_ext, slot_number), slot_faces(new_ext, slot_number)])
        for slot_number in range(MOST)
    ]
    rows = jnp.where(
        (dest_here & (dest_slot == 0))[:, None],
        slots[0].reshape(1, -1),
        jnp.where(dest_here[:, None], slots[1].reshape(1, -1), 0.0),
    )
    arrived = lax.all_to_all(rows.reshape(devices_fine, -1, 128), "fine", 0, 0, tiled=True)
    shell_pair = lax.dynamic_index_in_dim(arrived, source_of_mine, 0, keepdims=False)
    shell_pair = shell_pair.reshape(slots[0].shape)
    wide_pair = unpack_faces(shell_pair, cells_x)
    old_faces = [wide[0] for wide in wide_pair]
    mid_faces = [0.5 * (wide[0] + wide[1]) for wide in wide_pair]

    fine_box = fine_level[0, 0]
    fine_box = fine_advance(fine_box, old_faces, viscosity, reaction_rates, left_ids, right_ids)
    fine_box = fine_advance(fine_box, mid_faces, viscosity, reaction_rates, left_ids, right_ids)
    averaged = coarsen(fine_box)

    dest_ids = lax.broadcasted_iota(jnp.int32, (devices_fine, 1), 0)
    sent = jnp.where(dest_ids == source_of_mine, averaged.reshape(1, -1), 0.0)
    rows_in = lax.all_to_all(sent.reshape(devices_fine, -1, 128), "fine", 0, 0, tiled=True)
    y_ids = lax.broadcasted_iota(jnp.int32, (height, cells_z), 0)
    z_ids = lax.broadcasted_iota(jnp.int32, (height, cells_z), 1)
    coarse_out = coarse_next
    for slot_number in range(MOST):
        patch_id = slot_patch[slot_number]
        offset = y_cell[patch_id] - my_index * height
        z_start = z_cell[patch_id]
        incoming = lax.dynamic_index_in_dim(rows_in, owners[patch_id], 0, keepdims=False)
        incoming = incoming.reshape(averaged.shape)
        tiled = jnp.tile(incoming, (1, 1, height // BY, cells_z // BZ))
        covered = (
            slot_filled[slot_number]
            & (y_ids >= offset)
            & (y_ids < offset + BY)
            & (z_ids >= z_start)
            & (z_ids < z_start + BZ)
        )
        coarse_out = jnp.where(covered[None, None], tiled, coarse_out)
    return (coarse_out, fine_box[None, None])


def solution(mesh):
    placed = (
        P(None, "base", "fine", None),
        P("base", "fine", None, None, None, None),
        P("base", None, None),
        P("base", None),
        P(),
        P(),
        P(),
    )
    return jax.shard_map(
        per_device,
        mesh=mesh,
        in_specs=placed,
        out_specs=(P(None, "base", "fine", None), P("base", "fine", None, None, None, None)),
        check_vma=False,
    )
```
